256 devices in a mesh: seq: 256 (over y, z, x, core).
Axes of the slice: x: 4, y: 4, z: 8, core: 2. Of those that a mesh axis runs over, the one named last changes fastest.
Arguments:
- saved_input: bfloat16 [65536, 192], P('seq'), may hold values from -6 to 6
- cotangent: bfloat16 [65536, 192], P('seq'), may hold values from -15 to 15
- w_in: bfloat16 [384, 768], replicated, may hold values from -0.3125 to 0.3125
- bias_in: float32 [768], replicated, may hold values from -4 to 4
- w_out: bfloat16 [768, 384], replicated, may hold values from -0.21875 to 0.21875
- residual_logit: float32 [384], replicated, may hold values from -1 to 2
- branch_scale: float32 [384], replicated, may hold values from 0.1 to 1
Outputs:
- grad_input: bfloat16 [65536, 192], P('seq')
- grad_w_in: float32 [384, 768], replicated
- grad_w_out: float32 [768, 384], replicated
The draws below stay inside these ranges and needn't reach their ends.
All inputs are finite; a program needn't handle non-finite values.
Results may differ from the reference program's by a relative error of at most 0.02.
Values may be sent and summed in bfloat16 or wider, within the bound.
A program may use at most 64 MiB of HBM per device.

```python
import math
import jax
import jax.numpy as jnp
from jax import lax

WIDTH = 192
SWITCH_UNITS = 768
POS_DEV = 256
POSITIONS = 65536
LEVELS = 8


def draw_cotangent(key, part):
    position = jnp.arange(POSITIONS, dtype=jnp.float32) / POSITIONS
    row_scale = jnp.exp(jnp.log(16.0) * position) / 6.8
    base_draw = jnp.clip(jax.random.normal(key, (POSITIONS, WIDTH), jnp.float32), -6.0, 6.0)
    return (base_draw * row_scale[:, None]).astype(jnp.bfloat16)


def level_of(key, extent, pieces, smallest, high):
    def one(dim, blocks):
        draws = jax.random.uniform(jax.random.fold_in(jax.random.fold_in(key, 6), dim), (blocks,), jnp.float32, smallest / len(pieces), high / len(pieces))
        return jnp.repeat(jnp.exp(draws), extent[dim] // blocks).reshape((-1,) + (1,) * (len(extent) - dim - 1))

    level = one(*pieces[0])
    for cut in pieces[1:]:
        level = level * one(*cut)
    return level


def scatter_about(key, extent, width, reach, split=(), held_as=jnp.bfloat16):
    level = level_of(key, extent, split, -0.22, 0.18) if split else 1.0
    array = jax.random.normal(key, extent, jnp.float32) * width * level
    return jnp.minimum(jnp.maximum(array, -reach), reach).astype(held_as)


def setup_inputs(seed: int = 0) -> dict:
    key_of = jax.random.split(jax.random.key(seed), 8)
    return {
        "saved_input": scatter_about(key_of[0], (POSITIONS, WIDTH), 1.0, 6.0, ((0, 256),)),
        "cotangent": draw_cotangent(jax.random.fold_in(key_of[7], 71), 0),
        "w_in": scatter_about(key_of[2], (2 * WIDTH, SWITCH_UNITS), (2 * WIDTH) ** -0.5, 0.3125),
        "bias_in": scatter_about(key_of[3], (SWITCH_UNITS,), 1.0, 4.0, (), jnp.float32),
        "w_out": scatter_about(key_of[4], (SWITCH_UNITS, 2 * WIDTH), SWITCH_UNITS ** -0.5, 0.21875),
        "residual_logit": jnp.clip(jax.random.uniform(key_of[5], (2 * WIDTH,), jnp.float32, -1.0, 2.0), -1.0, 2.0),
        "branch_scale": jnp.clip(jnp.exp(jax.random.uniform(key_of[6], (2 * WIDTH,), jnp.float32, math.log(0.1), math.log(1.0))), 0.1, 1.0),
    }


epsilon = 1e-05
tanh_scale = 0.7978845608028654
cubic_coef = 0.044715

def gelu_slope(preact):
    inner = tanh_scale * (preact + cubic_coef * preact * preact * preact)
    tangent = jnp.tanh(inner)
    return 0.5 * (1.0 + tangent) + 0.5 * preact * (1.0 - tangent * tangent) * tanh_scale * (1.0 + 3.0 * cubic_coef * preact * preact)

def contract_rows(left, right):
    return lax.dot_general(left.astype(jnp.float32), right.astype(jnp.float32), (((0,), (0,)), ((), ())))

def switch_parts(paired, w_in, bias_in):
    values = paired.astype(jnp.float32)
    average = lax.optimization_barrier(jnp.mean(values, axis=-1, keepdims=True))
    centered = values - average
    inverse = lax.rsqrt(lax.optimization_barrier(jnp.mean(centered * centered, axis=-1, keepdims=True)) + epsilon)
    normed = centered * inverse
    normed_low = normed.astype(jnp.bfloat16)
    preact = jnp.dot(normed_low, w_in, preferred_element_type=jnp.float32) + bias_in
    activated = jax.nn.gelu(preact, approximate=True).astype(jnp.bfloat16)
    return (normed, normed_low, inverse, preact, activated)

def switch_result(paired, parts, w_out, keep_gate, branch_scale):
    branch = jnp.dot(parts[4], w_out, preferred_element_type=jnp.float32)
    return (keep_gate * paired.astype(jnp.float32) + branch_scale * branch).astype(jnp.bfloat16)

def switch_backward(pair_grad, parts, w_in, w_out, keep_gate, branch_scale):
    normed, normed_low, inverse, preact, activated = parts
    upstream = pair_grad.astype(jnp.float32)
    branch_grad = (branch_scale * upstream).astype(jnp.bfloat16)
    act_grad = jnp.dot(branch_grad, w_out.T, preferred_element_type=jnp.float32)
    preact_grad = (act_grad * gelu_slope(preact)).astype(jnp.bfloat16)
    normed_grad = jnp.dot(preact_grad, w_in.T, preferred_element_type=jnp.float32)
    centered_grad = normed_grad - lax.optimization_barrier(jnp.mean(normed_grad, axis=-1, keepdims=True)) - normed * lax.optimization_barrier(jnp.mean(normed_grad * normed, axis=-1, keepdims=True))
    input_grad = (keep_gate * upstream + inverse * centered_grad).astype(jnp.bfloat16)
    return (input_grad, normed_low, preact_grad, activated, branch_grad)

def pair_view(state, stride):
    groups = state.shape[0] // (2 * stride)
    viewed = state.reshape(groups, 2, stride, WIDTH)
    return jnp.concatenate([viewed[:, 0], viewed[:, 1]], axis=-1).reshape(groups * stride, 2 * WIDTH)

def unpair(paired, stride):
    groups = paired.shape[0] // stride
    viewed = paired.reshape(groups, stride, 2 * WIDTH)
    return jnp.stack([viewed[:, :, :WIDTH], viewed[:, :, WIDTH:]], axis=1).reshape(groups * 2 * stride, WIDTH)

def reference(saved_input, cotangent, w_in, bias_in, w_out, residual_logit, branch_scale):
    keep_gate = jax.nn.sigmoid(residual_logit)
    current = saved_input
    stored = []
    for level in range(LEVELS):
        stride = POS_DEV * 2 ** level
        paired = pair_view(current, stride)
        stored.append(paired)
        parts = switch_parts(paired, w_in, bias_in)
        current = unpair(switch_result(paired, parts, w_out, keep_gate, branch_scale), stride)
    grad_state = cotangent
    grad_in = jnp.zeros((2 * WIDTH, w_in.shape[1]), jnp.float32)
    grad_out = jnp.zeros((w_in.shape[1], 2 * WIDTH), jnp.float32)
    for level in reversed(range(LEVELS)):
        stride = POS_DEV * 2 ** level
        parts = switch_parts(stored[level], w_in, bias_in)
        input_grad, normed_low, preact_grad, activated, branch_grad = switch_backward(pair_view(grad_state, stride), parts, w_in, w_out, keep_gate, branch_scale)
        grad_state = unpair(input_grad, stride)
        grad_in = grad_in + contract_rows(normed_low, preact_grad)
        grad_out = grad_out + contract_rows(activated, branch_grad)
    grad_scale = POSITIONS ** (-0.5)
    return (grad_state, grad_in * grad_scale, grad_out * grad_scale)
```

```python
import functools

import jax
import jax.numpy as jnp
from jax import lax
from jax.experimental import pallas as pl
from jax.experimental.pallas import tpu as pltpu
from jax.sharding import PartitionSpec as P

epsilon = 1e-05
tanh_scale = 0.7978845608028654
cubic_coef = 0.044715
LANES = 128
PAD = 256
F32 = jnp.float32
BF16 = jnp.bfloat16


def row_dot(left, right):
    return jnp.dot(left, right, preferred_element_type=F32)


def column_dot(left, right):
    return lax.dot_general(left, right, (((0,), (0,)), ((), ())), preferred_element_type=F32)


def lanes_below(rows, lanes, bound):
    return lax.broadcasted_iota(jnp.int32, (rows, lanes), 1) < bound


def widen(values, width):
    rows = values.shape[0]
    keep = lanes_below(rows, PAD, width)
    first = jnp.where(keep, values[:, :PAD], 0.0)
    second = pltpu.roll(values[:, 2 * width - PAD :], width, 1)
    return jnp.concatenate([first, jnp.where(keep, second, 0.0)], axis=1)


def narrow(first, second, width):
    moved = pltpu.roll(second, width - LANES, 1)
    return jnp.concatenate([first[:, :LANES], first[:, LANES:] + moved[:, :LANES], moved[:, LANES:]], axis=1)


def halves(state, block):
    rows = state.shape[0]
    view = state.reshape(rows // (2 * block), 2, block, PAD)
    return view[:, 0].reshape(rows // 2, PAD), view[:, 1].reshape(rows // 2, PAD)


def unite(first, second, block):
    rows = first.shape[0]
    parts = [h.reshape(rows // block, 1, block, PAD) for h in (first, second)]
    return jnp.concatenate(parts, axis=1).reshape(2 * rows, PAD)


def kernel(
    dims, scale_out,
    x_ref, ct_ref, win_ref, bias_ref, wout_ref, logit_ref, scale_ref,
    gx_ref, grads_ref,
    ra, tb, rb, flat, wi, wit, wo, wot, gate, scale,
    nrm, inv, slope, nlc, act, pg, bgc,
    gb, rc, hsum, rd, rz, rg, tx, rx1, tx2, rx2,
    a_send, a_recv, b_send, b_recv, c_send, c_recv, d_send, d_recv, z_send, z_recv,
    e_send, e_recv, f_send, f_recv, u_send, u_recv, v_send, v_recv,
):
    ny, nz, nx, nc = dims
    nq, ns, npl = ny * nz, nx * nc, ny * nx
    rows, pairs = nq * ns, nq * ns // 2
    width = x_ref.shape[2]
    low_levels = ns.bit_length() - 1
    levels = rows.bit_length() - 1
    me = lax.axis_index("seq")
    q, s = me // ns, me % ns
    y, z, xc, c = q // nz, q % nz, s // nc, s % nc
    plane = y * nx + xc

    def id_qs(qq, ss):
        return qq * ns + ss

    def id_plane(pp):
        return (((pp // nx) * nz + z) * nx + pp % nx) * nc + c

    def id_z(zz):
        return ((y * nz + zz) * nx + xc) * nc + c

    sibling = id_qs(q, xc * nc + (1 - c))

    barrier = pltpu.get_barrier_semaphore()

    def greet(device):
        pl.semaphore_signal(barrier, inc=1, device_id=(device,), device_id_type=pl.DeviceIdType.MESH)

    @pl.loop(1, nq)
    def _(j):
        greet(id_qs((q + j) % nq, s))

    @pl.loop(1, ns)
    def _(j):
        greet(id_qs(q, (s + j) % ns))

    for jy in range(1, ny):
        for jx in range(1, nx):
            greet(id_plane(((y + jy) % ny) * nx + (xc + jx) % nx))
    pl.semaphore_wait(barrier, (nq - 1) + (ns - 1) + (ny - 1) * (nx - 1))

    def send(src, dst, send_sem, recv_sem, device):
        return pltpu.make_async_remote_copy(
            src_ref=src, dst_ref=dst, send_sem=send_sem, recv_sem=recv_sem,
            device_id=(device,), device_id_type=pl.DeviceIdType.MESH,
        )

    def exchange(count, place, src, dst, send_sem, recv_sem, device_of):
        def copy(j):
            to = (place + j) % count
            return send(src.at[to], dst.at[place], send_sem.at[j - 1], recv_sem.at[j - 1], device_of(to))

        def start():
            @pl.loop(1, count)
            def _(j):
                copy(j).start()

        def wait():
            @pl.loop(1, count)
            def _(j):
                copy(j).wait()

        return start, wait

    def start_a(k, src):
        start, wait = exchange(nq, q, src, ra.at[k], a_send.at[k], a_recv.at[k], lambda i: id_qs(i, s))
        start()
        ra[k, q] = src[q]
        return wait

    def put_rows(block):
        values = block.astype(F32).reshape(rows, width)
        flat[0] = values[:, :LANES]
        flat[1, :, : width - LANES] = values[:, LANES:]

    def strided(start, size, stride):
        return jnp.concatenate([flat[h, pl.ds(start, size, stride=stride), :] for h in range(2)], axis=1)

    def start_b(k):
        put_rows(ra[k])
        for r in range(ns):
            tb[k, r] = strided(r, nq, ns)[:, :width].astype(BF16)
        start, wait = exchange(ns, s, tb.at[k], rb.at[k], b_send.at[k], b_recv.at[k], lambda i: id_qs(q, i))
        start()
        rb[k, s] = tb[k, s]
        return wait

    flat[...] = jnp.zeros_like(flat)
    wait_a0 = start_a(0, x_ref)

    wide_in = jnp.zeros((PAD - width, win_ref.shape[1]), BF16)
    wi[:width] = win_ref[:width]
    wi[width:PAD] = wide_in
    wi[PAD : PAD + width] = win_ref[width:]
    wi[PAD + width :] = wide_in
    wit[...] = wi[...].T
    wo[...] = widen(wout_ref[...].astype(F32), width).astype(BF16)
    wot[...] = wo[...].T
    gate[...] = jax.nn.sigmoid(widen(jnp.broadcast_to(logit_ref[...], (8, 2 * width)), width))
    scale[...] = widen(jnp.broadcast_to(scale_ref[...], (8, 2 * width)), width)
    lane = lax.broadcasted_iota(jnp.int32, (1, 2 * PAD), 1) % PAD
    mask = jnp.where(lane < width, 1.0, 0.0)

    wait_a0()
    wait_b0 = start_b(0)
    wait_a1 = start_a(1, ct_ref)
    wait_b0()

    def load_state(k):
        put_rows(rb[k])
        return jnp.concatenate([flat[0], flat[1]], axis=1)

    def swap_order(state, major, minor):
        flat[0] = state[:, :LANES]
        flat[1] = state[:, LANES:]
        return jnp.concatenate([strided(j, major, minor) for j in range(minor)], axis=0)

    def block_of(level):
        return nq * 2**level if level < low_levels else 2**level

    state = load_state(0)
    for level in range(levels):
        if level == low_levels:
            state = swap_order(state, ns, nq)
            wait_a1()
            wait_b1 = start_b(1)
        first, second = halves(state, block_of(level))
        paired = jnp.concatenate([first, second], axis=1)
        average = jnp.sum(paired, axis=1, keepdims=True) * (1.0 / (2 * width))
        centered = paired - average * mask
        inverse = lax.rsqrt(jnp.sum(centered * centered, axis=1, keepdims=True) * (1.0 / (2 * width)) + epsilon)
        normed = centered * inverse
        nrm[level] = normed
        inv[level] = inverse
        here = pl.ds(level * pairs, pairs)
        nlc[here, :] = narrow(normed[:, :PAD], normed[:, PAD:], width).astype(BF16)
        preact = row_dot(normed.astype(BF16), wi[...]) + bias_ref[...]
        square = preact * preact
        tangent = jnp.tanh(preact * (tanh_scale + (tanh_scale * cubic_coef) * square))
        half = 0.5 + 0.5 * tangent
        activated = (preact * half).astype(BF16)
        act[here, :] = activated
        slope[level] = half + (0.5 * preact) * (1.0 - tangent * tangent) * (
            tanh_scale + (3.0 * tanh_scale * cubic_coef) * square
        )
        if level + 1 < levels:
            result = gate[0:1] * paired + scale[0:1] * row_dot(activated, wo[...])
            state = unite(result[:, :PAD], result[:, PAD:], block_of(level))

    wait_b1()
    state = swap_order(load_state(1), ns, nq)
    for level in reversed(range(levels)):
        if level == low_levels - 1:
            state = swap_order(state, nq, ns)
        first, second = halves(state, block_of(level))
        upstream = jnp.concatenate([first, second], axis=1)
        branch = scale[0:1] * upstream
        here = pl.ds(level * pairs, pairs)
        bgc[here, :] = narrow(branch[:, :PAD], branch[:, PAD:], width).astype(BF16)
        preact_grad = (row_dot(branch.astype(BF16), wot[...]) * slope[level]).astype(BF16)
        pg[here, :] = preact_grad
        normed_grad = row_dot(preact_grad, wit[...])
        normed = nrm[level]
        mean_grad = jnp.sum(normed_grad, axis=1, keepdims=True) * (1.0 / (2 * width))
        mean_both = jnp.sum(normed_grad * normed, axis=1, keepdims=True) * (1.0 / (2 * width))
        grad = gate[0:1] * upstream + inv[level] * (normed_grad - mean_grad * mask - normed * mean_both)
        state = unite(grad[:, :PAD], grad[:, PAD:], block_of(level))

    tx[...] = state[:, :width].reshape(ns, nq, width).astype(BF16)
    start_u, wait_u = exchange(ns, s, tx, rx1, u_send, u_recv, lambda i: id_qs(q, i))
    start_u()
    rx1[s] = tx[s]

    units = act.shape[1]
    piece = gb.shape[2]
    span = 2 * width
    count = span // piece
    for h in range(units // span):
        block = pl.ds(h * span, span)
        grad_in = column_dot(nlc[...], pg[:, block])
        gb[0, pl.ds(h * count, count)] = grad_in.reshape(count, piece, span).astype(BF16)
    for h in range(units // span):
        block = pl.ds(h * span, span)
        grad_out = column_dot(act[:, block], bgc[...])
        gb[1, pl.ds(h * count, count)] = grad_out.reshape(count, piece, span).astype(BF16)

    copy_c = send(gb.at[1 - c], rc, c_send, c_recv, sibling)
    copy_c.start()

    wait_u()
    put_rows(rx1[...])
    for j in range(nq):
        tx2[j] = strided(j, ns, nq)[:, :width].astype(BF16)
    start_v, wait_v = exchange(nq, q, tx2, rx2, v_send, v_recv, lambda i: id_qs(i, s))
    start_v()
    rx2[q] = tx2[q]

    copy_c.wait()
    hsum[...] = (gb[c].astype(F32) + rc[...].astype(F32)).astype(BF16)

    start_d, wait_d = exchange(npl, plane, hsum, rd, d_send, d_recv, id_plane)
    start_d()
    rd[plane] = hsum[plane]
    wait_d()
    total = rd[0].astype(F32)
    for i in range(1, npl):
        total = total + rd[i].astype(F32)
    rz[z] = total.astype(BF16)

    def copy_z(j):
        return send(rz.at[z], rz.at[z], z_send.at[j - 1], z_recv.at[j - 1], id_z((z + j) % nz))

    @pl.loop(1, nz)
    def _(j):
        copy_z(j).start()

    @pl.loop(1, nz)
    def _(j):
        copy_z(j).wait()

    total = rz[0].astype(F32)
    for i in range(1, nz):
        total = total + rz[i].astype(F32)
    rg[c, plane] = (total * scale_out).astype(BF16)

    def copy_e(j):
        mine = rg.at[c, plane]
        return send(mine, mine, e_send.at[j - 1], e_recv.at[j - 1], id_plane((plane + j) % npl))

    @pl.loop(1, npl)
    def _(j):
        copy_e(j).start()

    @pl.loop(1, npl)
    def _(j):
        copy_e(j).wait()

    copy_f = send(rg.at[c], rg.at[c], f_send, f_recv, sibling)
    copy_f.start()
    wait_v()
    gx_ref[...] = rx2[...]
    copy_f.wait()
    grads_ref[...] = rg[...]


def build(mesh, dims, interpret=False):
    ny, nz, nx, nc = dims
    nq, ns, npl = ny * nz, nx * nc, ny * nx
    rows, pairs = nq * ns, nq * ns // 2
    levels = rows.bit_length() - 1

    def step(saved_input, cotangent, w_in, bias_in, w_out, residual_logit, branch_scale):
        width, units = saved_input.shape[1], w_in.shape[1]
        piece = units // npl
        span = 2 * width
        vmem = pltpu.VMEM
        dma = pltpu.SemaphoreType.DMA
        scratch = [
            vmem((2, nq, ns, width), BF16),
            vmem((2, ns, nq, width), BF16),
            vmem((2, ns, nq, width), BF16),
            vmem((2, rows, LANES), F32),
            vmem((2 * PAD, units), BF16),
            vmem((units, 2 * PAD), BF16),
            vmem((units, 2 * PAD), BF16),
            vmem((2 * PAD, units), BF16),
            vmem((8, 2 * PAD), F32),
            vmem((8, 2 * PAD), F32),
            vmem((levels, pairs, 2 * PAD), F32),
            vmem((levels, pairs, 1), F32),
            vmem((levels, pairs, units), F32),
            vmem((levels * pairs, span), BF16),
            vmem((levels * pairs, units), BF16),
            vmem((levels * pairs, units), BF16),
            vmem((levels * pairs, span), BF16),
            vmem((2, npl, piece, span), BF16),
            vmem((npl, piece, span), BF16),
            vmem((npl, piece, span), BF16),
            vmem((npl, piece, span), BF16),
            vmem((nz, piece, span), BF16),
            vmem((2, npl, piece, span), BF16),
            vmem((ns, nq, width), BF16),
            vmem((ns, nq, width), BF16),
            vmem((nq, ns, width), BF16),
            vmem((nq, ns, width), BF16),
            dma((2, nq - 1)), dma((2, nq - 1)),
            dma((2, ns - 1)), dma((2, ns - 1)),
            dma, dma,
            dma((npl - 1,)), dma((npl - 1,)),
            dma((nz - 1,)), dma((nz - 1,)),
            dma((npl - 1,)), dma((npl - 1,)),
            dma, dma,
            dma((ns - 1,)), dma((ns - 1,)),
            dma((nq - 1,)), dma((nq - 1,)),
        ]
        in_vmem = pl.BlockSpec(memory_space=pltpu.VMEM)
        gx, grads = pl.pallas_call(
            functools.partial(kernel, dims, float(rows * rows) ** (-0.5)),
            out_shape=(
                jax.ShapeDtypeStruct((nq, ns, width), BF16),
                jax.ShapeDtypeStruct((2, npl, piece, span), BF16),
            ),
            in_specs=[in_vmem] * 7,
            out_specs=(in_vmem, in_vmem),
            scratch_shapes=scratch,
            compiler_params=pltpu.CompilerParams(collective_id=0, has_side_effects=True, vmem_limit_bytes=60 * 2**20),
        )(
            saved_input.reshape(nq, ns, width), cotangent.reshape(nq, ns, width), w_in, bias_in.reshape(1, units),
            w_out, residual_logit.reshape(1, span), branch_scale.reshape(1, span),
        )
        parts = grads.reshape(2, units // span, span, span).astype(F32)
        grad_in = parts[0].transpose(1, 0, 2).reshape(span, units)
        grad_out = parts[1].reshape(units, span)
        return gx.reshape(rows, width), grad_in, grad_out

    in_specs = (P("seq", None), P("seq", None), P(), P(), P(), P(), P())
    out_specs = (P("seq", None), P(), P())
    return jax.shard_map(step, mesh=mesh, in_specs=in_specs, out_specs=out_specs, check_vma=False)


def solution(mesh):
    return build(mesh, (4, 8, 4, 2))
```

```python
import functools

import jax
import jax.numpy as jnp
from jax import lax
from jax.experimental import pallas as pl
from jax.experimental.pallas import tpu as pltpu
from jax.sharding import PartitionSpec as P

epsilon = 1e-05
tanh_scale = 0.7978845608028654
cubic_coef = 0.044715
LANES = 128
PAD = 256
F32 = jnp.float32
BF16 = jnp.bfloat16


def row_dot(left, right):
    return jnp.dot(left, right, preferred_element_type=F32)


def column_dot(left, right):
    return lax.dot_general(left, right, (((0,), (0,)), ((), ())), preferred_element_type=F32)


def lanes_below(rows, lanes, bound):
    return lax.broadcasted_iota(jnp.int32, (rows, lanes), 1) < bound


def widen(values, width):
    rows = values.shape[0]
    keep = lanes_below(rows, PAD, width)
    first = jnp.where(keep, values[:, :PAD], 0.0)
    second = pltpu.roll(values[:, 2 * width - PAD :], width, 1)
    return jnp.concatenate([first, jnp.where(keep, second, 0.0)], axis=1)


def narrow(first, second, width):
    moved = pltpu.roll(second, width - LANES, 1)
    return jnp.concatenate([first[:, :LANES], first[:, LANES:] + moved[:, :LANES], moved[:, LANES:]], axis=1)


def halves(state, block):
    rows = state.shape[0]
    view = state.reshape(rows // (2 * block), 2, block, PAD)
    return view[:, 0].reshape(rows // 2, PAD), view[:, 1].reshape(rows // 2, PAD)


def unite(first, second, block):
    rows = first.shape[0]
    parts = [h.reshape(rows // block, 1, block, PAD) for h in (first, second)]
    return jnp.concatenate(parts, axis=1).reshape(2 * rows, PAD)


def kernel(
    dims, scale_out,
    xt_hbm, ct_hbm, win_hbm, bias_hbm, wout_hbm, logit_hbm, scale_hbm,
    gx_ref, grads_ref,
    xt, win, bias_row, wout, logit_row, scale_row, xs,
    ra, tb, rb, flat, wi, wit, wo, wot, gate, scale,
    nrm, inv, slope, nlc, act, pg, bgc,
    gb, rc, hsum, rd, rz, rg, tx, rx1, tx2, rx2,
    load_sem, a_send, a_recv, b_send, b_recv, c_send, c_recv, d_send, d_recv, z_send, z_recv,
    e_send, e_recv, f_send, f_recv, u_send, u_recv, v_send, v_recv,
):
    ny, nz, nx, nc = dims
    nq, ns, npl = ny * nz, nx * nc, ny * nx
    rows, pairs = nq * ns, nq * ns // 2
    width = xt.shape[1]
    low_levels = ns.bit_length() - 1
    levels = rows.bit_length() - 1
    me = lax.axis_index("seq")
    q, s = me // ns, me % ns
    y, z, xc, c = q // nz, q % nz, s // nc, s % nc
    plane = y * nx + xc

    def id_qs(qq, ss):
        return qq * ns + ss

    def id_plane(pp):
        return (((pp // nx) * nz + z) * nx + pp % nx) * nc + c

    def id_z(zz):
        return ((y * nz + zz) * nx + xc) * nc + c

    sibling = id_qs(q, xc * nc + (1 - c))

    barrier = pltpu.get_barrier_semaphore()

    def greet(device):
        pl.semaphore_signal(barrier, inc=1, device_id=(device,), device_id_type=pl.DeviceIdType.MESH)

    @pl.loop(1, nq)
    def _(j):
        greet(id_qs((q + j) % nq, s))

    @pl.loop(1, ns)
    def _(j):
        greet(id_qs(q, (s + j) % ns))

    for jy in range(1, ny):
        for jx in range(1, nx):
            greet(id_plane(((y + jy) % ny) * nx + (xc + jx) % nx))

    operands = (
        (xt_hbm, xt.at[0]), (ct_hbm, xt.at[1]), (logit_hbm, logit_row), (scale_hbm, scale_row), (bias_hbm, bias_row),
        (win_hbm, win), (wout_hbm, wout),
    )
    loads = [pltpu.make_async_copy(src, dst, load_sem.at[i]) for i, (src, dst) in enumerate(operands)]
    for load in loads:
        load.start()
    flat[...] = jnp.zeros_like(flat)
    for k in range(2):
        loads[k].wait()
        xs[k] = xt[k].T.reshape(nq, ns, width)
    for load in loads[2:]:
        load.wait()
    wide_in = jnp.zeros((PAD - width, win.shape[1]), BF16)
    wi[:width] = win[:width]
    wi[width:PAD] = wide_in
    wi[PAD : PAD + width] = win[width:]
    wi[PAD + width :] = wide_in
    wit[...] = wi[...].T
    wo[...] = widen(wout[...].astype(F32), width).astype(BF16)
    wot[...] = wo[...].T
    gate[...] = jax.nn.sigmoid(widen(jnp.broadcast_to(logit_row[...].reshape(1, 2 * width), (8, 2 * width)), width))
    scale[...] = widen(jnp.broadcast_to(scale_row[...].reshape(1, 2 * width), (8, 2 * width)), width)
    bias = bias_row[...].reshape(1, bias_row.shape[0])
    lane = lax.broadcasted_iota(jnp.int32, (1, 2 * PAD), 1) % PAD
    mask = jnp.where(lane < width, 1.0, 0.0)

    pl.semaphore_wait(barrier, (nq - 1) + (ns - 1) + (ny - 1) * (nx - 1))

    def send(src, dst, send_sem, recv_sem, device):
        return pltpu.make_async_remote_copy(
            src_ref=src, dst_ref=dst, send_sem=send_sem, recv_sem=recv_sem,
            device_id=(device,), device_id_type=pl.DeviceIdType.MESH,
        )

    def each(count, copy):
        def start():
            @pl.loop(1, count)
            def _(j):
                copy(j).start()

        def wait():
            @pl.loop(1, count)
            def _(j):
                copy(j).wait()

        return start, wait

    def exchange(count, place, src, dst, send_sem, recv_sem, device_of):
        def copy(j):
            to = (place + j) % count
            return send(src.at[to], dst.at[place], send_sem.at[j - 1], recv_sem.at[j - 1], device_of(to))

        return each(count, copy)

    def spread(count, place, ref, send_sem, recv_sem, device_of):
        def copy(j):
            to = (place + j) % count
            return send(ref.at[place], ref.at[place], send_sem.at[j - 1], recv_sem.at[j - 1], device_of(to))

        return each(count, copy)

    def start_a(k):
        start, wait = exchange(nq, q, xs.at[k], ra.at[k], a_send.at[k], a_recv.at[k], lambda i: id_qs(i, s))
        start()
        ra[k, q] = xs[k, q]
        return wait

    def put_rows(block):
        values = block.astype(F32).reshape(rows, width)
        flat[0] = values[:, :LANES]
        flat[1, :, : width - LANES] = values[:, LANES:]

    def strided(start, size, stride):
        return jnp.concatenate([flat[h, pl.ds(start, size, stride=stride), :] for h in range(2)], axis=1)

    def start_b(k):
        put_rows(ra[k])
        for r in range(ns):
            tb[k, r] = strided(r, nq, ns)[:, :width].astype(BF16)
        start, wait = exchange(ns, s, tb.at[k], rb.at[k], b_send.at[k], b_recv.at[k], lambda i: id_qs(q, i))
        start()
        rb[k, s] = tb[k, s]
        return wait

    wait_a0 = start_a(0)
    wait_a1 = start_a(1)
    wait_a0()
    wait_b0 = start_b(0)
    wait_a1()
    wait_b1 = start_b(1)
    wait_b0()

    def load_state(k):
        put_rows(rb[k])
        return jnp.concatenate([flat[0], flat[1]], axis=1)

    def swap_order(state, major, minor):
        flat[0] = state[:, :LANES]
        flat[1] = state[:, LANES:]
        return jnp.concatenate([strided(j, major, minor) for j in range(minor)], axis=0)

    def block_of(level):
        return nq * 2**level if level < low_levels else 2**level

    state = load_state(0)
    for level in range(levels):
        if level == low_levels:
            state = swap_order(state, ns, nq)
        first, second = halves(state, block_of(level))
        paired = jnp.concatenate([first, second], axis=1)
        average = jnp.sum(paired, axis=1, keepdims=True) * (1.0 / (2 * width))
        centered = paired - average * mask
        inverse = lax.rsqrt(jnp.sum(centered * centered, axis=1, keepdims=True) * (1.0 / (2 * width)) + epsilon)
        normed = centered * inverse
        nrm[level] = normed
        inv[level] = inverse
        here = pl.ds(level * pairs, pairs)
        nlc[here, :] = narrow(normed[:, :PAD], normed[:, PAD:], width).astype(BF16)
        preact = row_dot(normed.astype(BF16), wi[...]) + bias
        square = preact * preact
        tangent = jnp.tanh(preact * (tanh_scale + (tanh_scale * cubic_coef) * square))
        half = 0.5 + 0.5 * tangent
        activated = (preact * half).astype(BF16)
        act[here, :] = activated
        slope[level] = half + (0.5 * preact) * (1.0 - tangent * tangent) * (
            tanh_scale + (3.0 * tanh_scale * cubic_coef) * square
        )
        if level + 1 < levels:
            result = gate[0:1] * paired + scale[0:1] * row_dot(activated, wo[...])
            state = unite(result[:, :PAD], result[:, PAD:], block_of(level))

    wait_b1()
    state = swap_order(load_state(1), ns, nq)
    for level in reversed(range(levels)):
        if level == low_levels - 1:
            state = swap_order(state, nq, ns)
        first, second = halves(state, block_of(level))
        upstream = jnp.concatenate([first, second], axis=1)
        branch = scale[0:1] * upstream
        here = pl.ds(level * pairs, pairs)
        bgc[here, :] = narrow(branch[:, :PAD], branch[:, PAD:], width).astype(BF16)
        preact_grad = (row_dot(branch.astype(BF16), wot[...]) * slope[level]).astype(BF16)
        pg[here, :] = preact_grad
        normed_grad = row_dot(preact_grad, wit[...])
        normed = nrm[level]
        mean_grad = jnp.sum(normed_grad, axis=1, keepdims=True) * (1.0 / (2 * width))
        mean_both = jnp.sum(normed_grad * normed, axis=1, keepdims=True) * (1.0 / (2 * width))
        grad = gate[0:1] * upstream + inv[level] * (normed_grad - mean_grad * mask - normed * mean_both)
        state = unite(grad[:, :PAD], grad[:, PAD:], block_of(level))

    tx[...] = state[:, :width].reshape(ns, nq, width).astype(BF16)
    start_u, wait_u = exchange(ns, s, tx, rx1, u_send, u_recv, lambda i: id_qs(q, i))
    start_u()
    rx1[s] = tx[s]

    chunks = gb.shape[1]
    span = 2 * width
    units = act.shape[1]
    in_rows, out_rows = span // chunks, units // chunks
    to_sibling = []
    for k in range(chunks):
        grad_in = column_dot(nlc[:, k * in_rows : (k + 1) * in_rows], pg[...])
        for h in range(2):
            gb[0, k, :, h] = grad_in[:, h * span : (h + 1) * span].reshape(npl, 8, span).astype(BF16)
        grad_out = column_dot(act[:, k * out_rows : (k + 1) * out_rows], bgc[...])
        gb[1, k] = grad_out.reshape(npl, 2, 8, span).astype(BF16)
        to_sibling.append(send(gb.at[1 - c, k], rc.at[k], c_send.at[k], c_recv.at[k], sibling))
        to_sibling[k].start()

    plane_waits = []
    for k in range(chunks):
        to_sibling[k].wait()
        hsum[k] = (gb[c, k].astype(F32) + rc[k].astype(F32)).astype(BF16)
        start, wait = exchange(npl, plane, hsum.at[k], rd.at[k], d_send.at[k], d_recv.at[k], id_plane)
        start()
        plane_waits.append(wait)
        rd[k, plane] = hsum[k, plane]

    wait_u()
    put_rows(rx1[...])
    for j in range(nq):
        tx2[j] = strided(j, ns, nq)[:, :width].astype(BF16)
    start_v, wait_v = exchange(nq, q, tx2, rx2, v_send, v_recv, lambda i: id_qs(i, s))
    start_v()
    rx2[q] = tx2[q]

    def added(ref, count):
        total = ref[0].astype(F32)
        for i in range(1, count):
            total = total + ref[i].astype(F32)
        return total

    z_waits = []
    for k in range(chunks):
        plane_waits[k]()
        rz[k, z] = added(rd.at[k], npl).astype(BF16)
        start, wait = spread(nz, z, rz.at[k], z_send.at[k], z_recv.at[k], id_z)
        start()
        z_waits.append(wait)

    gather_waits = []
    for k in range(chunks):
        z_waits[k]()
        rg[c, k, plane] = (added(rz.at[k], nz) * scale_out).astype(BF16)
        start, wait = spread(npl, plane, rg.at[c, k], e_send.at[k], e_recv.at[k], id_plane)
        start()
        gather_waits.append(wait)
    over = []
    for k in range(chunks):
        gather_waits[k]()
        over.append(send(rg.at[c, k], rg.at[c, k], f_send.at[k], f_recv.at[k], sibling))
        over[k].start()
    wait_v()
    gx_ref[...] = rx2[...]
    for k in range(chunks):
        over[k].wait()
        grads_ref[:, k] = rg[:, k]


def finish(gx_ref, grads_ref, gxt_ref, gin_ref, gout_ref):
    @pl.when(pl.program_id(0) == 0)
    def _():
        rows = gx_ref.shape[0] * gx_ref.shape[1]
        gxt_ref[...] = gx_ref[...].reshape(rows, gx_ref.shape[2]).T

    span = gout_ref.shape[1]
    for h in range(2):
        gin_ref[:, h * span : (h + 1) * span] = grads_ref[0, 0, :, h].astype(F32).reshape(gin_ref.shape[0], span)
    gout_ref[...] = grads_ref[1, 0].astype(F32).reshape(gout_ref.shape)


def build(mesh, dims):
    ny, nz, nx, nc = dims
    nq, ns, npl = ny * nz, nx * nc, ny * nx
    rows, pairs = nq * ns, nq * ns // 2
    levels = rows.bit_length() - 1

    def step(saved_input, cotangent, w_in, bias_in, w_out, residual_logit, branch_scale):
        width, units = saved_input.shape[1], w_in.shape[1]
        span = 2 * width
        chunks = span // (npl * 8)
        vmem = pltpu.VMEM
        dma = pltpu.SemaphoreType.DMA
        scratch = [
            vmem((2, width, rows), BF16),
            vmem((span, units), BF16),
            vmem((units,), F32),
            vmem((units, span), BF16),
            vmem((span,), F32),
            vmem((span,), F32),
            vmem((2, nq, ns, width), BF16),
            vmem((2, nq, ns, width), BF16),
            vmem((2, ns, nq, width), BF16),
            vmem((2, ns, nq, width), BF16),
            vmem((2, rows, LANES), F32),
            vmem((2 * PAD, units), BF16),
            vmem((units, 2 * PAD), BF16),
            vmem((units, 2 * PAD), BF16),
            vmem((2 * PAD, units), BF16),
            vmem((8, 2 * PAD), F32),
            vmem((8, 2 * PAD), F32),
            vmem((levels, pairs, 2 * PAD), F32),
            vmem((levels, pairs, 1), F32),
            vmem((levels, pairs, units), F32),
            vmem((levels * pairs, span), BF16),
            vmem((levels * pairs, units), BF16),
            vmem((levels * pairs, units), BF16),
            vmem((levels * pairs, span), BF16),
            vmem((2, chunks, npl, 2, 8, span), BF16),
            vmem((chunks, npl, 2, 8, span), BF16),
            vmem((chunks, npl, 2, 8, span), BF16),
            vmem((chunks, npl, 2, 8, span), BF16),
            vmem((chunks, nz, 2, 8, span), BF16),
            vmem((2, chunks, npl, 2, 8, span), BF16),
            vmem((ns, nq, width), BF16),
            vmem((ns, nq, width), BF16),
            vmem((nq, ns, width), BF16),
            vmem((nq, ns, width), BF16),
            dma((7,)),
            dma((2, nq - 1)), dma((2, nq - 1)),
            dma((2, ns - 1)), dma((2, ns - 1)),
            dma((chunks,)), dma((chunks,)),
            dma((chunks, npl - 1)), dma((chunks, npl - 1)),
            dma((chunks, nz - 1)), dma((chunks, nz - 1)),
            dma((chunks, npl - 1)), dma((chunks, npl - 1)),
            dma((chunks,)), dma((chunks,)),
            dma((ns - 1,)), dma((ns - 1,)),
            dma((nq - 1,)), dma((nq - 1,)),
        ]
        in_vmem = pl.BlockSpec(memory_space=pltpu.VMEM)
        gx, grads = pl.pallas_call(
            functools.partial(kernel, dims, float(rows * rows) ** (-0.5)),
            out_shape=(
                jax.ShapeDtypeStruct((nq, ns, width), BF16),
                jax.ShapeDtypeStruct((2, chunks, npl, 2, 8, span), BF16),
            ),
            in_specs=[pl.BlockSpec(memory_space=pl.ANY)] * 7,
            out_specs=(in_vmem, in_vmem),
            scratch_shapes=scratch,
            compiler_params=pltpu.CompilerParams(collective_id=0, has_side_effects=True, vmem_limit_bytes=60 * 2**20),
        )(saved_input.T, cotangent.T, w_in, bias_in, w_out, residual_logit, branch_scale)
        gxt, grad_in, grad_out = pl.pallas_call(
            finish,
            grid=(chunks,),
            out_shape=(
                jax.ShapeDtypeStruct((width, rows), BF16),
                jax.ShapeDtypeStruct((span, units), F32),
                jax.ShapeDtypeStruct((units, span), F32),
            ),
            in_specs=[
                pl.BlockSpec((nq, ns, width), lambda k: (0, 0, 0)),
                pl.BlockSpec((2, 1, npl, 2, 8, span), lambda k: (0, k, 0, 0, 0, 0)),
            ],
            out_specs=(
                pl.BlockSpec((width, rows), lambda k: (0, 0)),
                pl.BlockSpec((span // chunks, units), lambda k: (k, 0)),
                pl.BlockSpec((units // chunks, span), lambda k: (k, 0)),
            ),
        )(gx, grads)
        return gxt.T, grad_in, grad_out

    in_specs = (P("seq", None), P("seq", None), P(), P(), P(), P(), P())
    out_specs = (P("seq", None), P(), P())
    return jax.shard_map(step, mesh=mesh, in_specs=in_specs, out_specs=out_specs, check_vma=False)


def solution(mesh):
    return build(mesh, (4, 8, 4, 2))
```

```python
import functools

import jax
import jax.numpy as jnp
from jax import lax
from jax.experimental import pallas as pl
from jax.experimental.pallas import tpu as pltpu
from jax.sharding import PartitionSpec as P

epsilon = 1e-05
tanh_scale = 0.7978845608028654
cubic_coef = 0.044715
LANES = 128
PAD = 256
F32 = jnp.float32
BF16 = jnp.bfloat16


def row_dot(left, right):
    return jnp.dot(left, right, preferred_element_type=F32)


def column_dot(left, right):
    return lax.dot_general(left, right, (((0,), (0,)), ((), ())), preferred_element_type=F32)


def lanes_below(rows, lanes, bound):
    return lax.broadcasted_iota(jnp.int32, (rows, lanes), 1) < bound


def widen(values, width):
    rows = values.shape[0]
    keep = lanes_below(rows, PAD, width)
    first = jnp.where(keep, values[:, :PAD], 0.0)
    second = pltpu.roll(values[:, 2 * width - PAD :], width, 1)
    return jnp.concatenate([first, jnp.where(keep, second, 0.0)], axis=1)


def narrow(first, second, width):
    moved = pltpu.roll(second, width - LANES, 1)
    return jnp.concatenate([first[:, :LANES], first[:, LANES:] + moved[:, :LANES], moved[:, LANES:]], axis=1)


def halves(state, block):
    rows = state.shape[0]
    view = state.reshape(rows // (2 * block), 2, block, PAD)
    return view[:, 0].reshape(rows // 2, PAD), view[:, 1].reshape(rows // 2, PAD)


def unite(first, second, block):
    rows = first.shape[0]
    parts = [h.reshape(rows // block, 1, block, PAD) for h in (first, second)]
    return jnp.concatenate(parts, axis=1).reshape(2 * rows, PAD)


def kernel(
    dims, scale_out,
    xt_hbm, ct_hbm, win_hbm, bias_hbm, wout_hbm, logit_hbm, scale_hbm,
    gx_out, grads_out,
    xt, win, bias_row, wout, logit_row, scale_row, xs,
    ra, tb, rb, flat, wi, wit, wo, wot, gate, scale,
    nrm, inv, slope, nlc, act, pg, bgc,
    gb, rc, hsum, rd, rz, rg, tx, rx1, tx2, rx2,
    load_sem, a_send, a_recv, b_send, b_recv, c_send, c_recv, d_send, d_recv, z_send, z_recv,
    e_send, e_recv, f_send, f_recv, u_send, u_recv, v_send, v_recv, out_sem,
):
    ny, nz, nx, nc = dims
    nq, ns, npl = ny * nz, nx * nc, ny * nx
    rows, pairs = nq * ns, nq * ns // 2
    width = xt.shape[1]
    low_levels = ns.bit_length() - 1
    levels = rows.bit_length() - 1
    me = lax.axis_index("seq")
    q, s = lax.div(me, ns), lax.rem(me, ns)
    y, z, xc, c = lax.div(q, nz), lax.rem(q, nz), lax.div(s, nc), lax.rem(s, nc)
    plane = y * nx + xc

    def id_qs(qq, ss):
        return qq * ns + ss

    def id_plane(pp):
        return ((lax.div(pp, nx) * nz + z) * nx + lax.rem(pp, nx)) * nc + c

    def id_z(zz):
        return ((y * nz + zz) * nx + xc) * nc + c

    sibling = id_qs(q, xc * nc + (1 - c))

    barrier = pltpu.get_barrier_semaphore()

    def greet(device):
        pl.semaphore_signal(barrier, inc=1, device_id=(device,), device_id_type=pl.DeviceIdType.MESH)

    @pl.loop(1, nq)
    def _(j):
        greet(id_qs(lax.rem(q + j, nq), s))

    @pl.loop(1, ns)
    def _(j):
        greet(id_qs(q, lax.rem(s + j, ns)))

    for jy in range(1, ny):
        for jx in range(1, nx):
            greet(((lax.rem(y + jy, ny) * nz + z) * nx + lax.rem(xc + jx, nx)) * nc + c)

    operands = (
        (xt_hbm, xt.at[0]), (ct_hbm, xt.at[1]), (logit_hbm, logit_row), (scale_hbm, scale_row), (bias_hbm, bias_row),
        (win_hbm, win), (wout_hbm, wout),
    )
    loads = [pltpu.make_async_copy(src, dst, load_sem.at[i]) for i, (src, dst) in enumerate(operands)]
    for load in loads:
        load.start()
    flat[...] = jnp.zeros_like(flat)
    for k in range(2):
        loads[k].wait()
        xs[k] = xt[k].T.reshape(nq, ns, width)
    for load in loads[2:]:
        load.wait()
    wide_in = jnp.zeros((PAD - width, win.shape[1]), BF16)
    wi[:width] = win[:width]
    wi[width:PAD] = wide_in
    wi[PAD : PAD + width] = win[width:]
    wi[PAD + width :] = wide_in
    wit[...] = wi[...].T
    wo[...] = widen(wout[...].astype(F32), width).astype(BF16)
    wot[...] = wo[...].T
    gate[...] = jax.nn.sigmoid(widen(jnp.broadcast_to(logit_row[...].reshape(1, 2 * width), (8, 2 * width)), width))
    scale[...] = widen(jnp.broadcast_to(scale_row[...].reshape(1, 2 * width), (8, 2 * width)), width)
    bias = bias_row[...].reshape(1, bias_row.shape[0])
    lane = lax.broadcasted_iota(jnp.int32, (1, 2 * PAD), 1) % PAD
    mask = jnp.where(lane < width, 1.0, 0.0)

    pl.semaphore_wait(barrier, (nq - 1) + (ns - 1) + (ny - 1) * (nx - 1))

    def send(src, dst, send_sem, recv_sem, device):
        return pltpu.make_async_remote_copy(
            src_ref=src, dst_ref=dst, send_sem=send_sem, recv_sem=recv_sem,
            device_id=(device,), device_id_type=pl.DeviceIdType.MESH,
        )

    def bytes_of(ref, sem):
        return pltpu.make_async_copy(ref, ref, sem)

    def each(count, copy, landing, recv_sem):
        def start():
            @pl.loop(1, count)
            def _(j):
                copy(j).start()

        return start, bytes_of(landing.at[pl.ds(0, count - 1)], recv_sem).wait

    def exchange(count, place, src, dst, send_sem, recv_sem, device_of):
        def copy(j):
            to = lax.rem(place + j, count)
            return send(src.at[to], dst.at[place], send_sem, recv_sem, device_of(to))

        return each(count, copy, dst, recv_sem)

    def spread(count, place, ref, send_sem, recv_sem, device_of):
        def copy(j):
            return send(ref.at[place], ref.at[place], send_sem, recv_sem, device_of(lax.rem(place + j, count)))

        return each(count, copy, ref, recv_sem)

    def start_a(k):
        start, wait = exchange(nq, q, xs.at[k], ra.at[k], a_send, a_recv.at[k], lambda i: id_qs(i, s))
        start()
        ra[k, q] = xs[k, q]
        return wait

    def put_rows(block):
        values = block.astype(F32).reshape(rows, width)
        flat[0] = values[:, :LANES]
        flat[1, :, : width - LANES] = values[:, LANES:]

    def strided(start, size, stride):
        return jnp.concatenate([flat[h, pl.ds(start, size, stride=stride), :] for h in range(2)], axis=1)

    def start_b(k):
        put_rows(ra[k])
        for r in range(ns):
            tb[k, r] = strided(r, nq, ns)[:, :width].astype(BF16)
        start, wait = exchange(ns, s, tb.at[k], rb.at[k], b_send, b_recv.at[k], lambda i: id_qs(q, i))
        start()
        rb[k, s] = tb[k, s]
        return wait

    wait_a0 = start_a(0)
    wait_a1 = start_a(1)
    wait_a0()
    wait_b0 = start_b(0)
    wait_a1()
    wait_b1 = start_b(1)
    wait_b0()

    def load_state(k):
        put_rows(rb[k])
        return jnp.concatenate([flat[0], flat[1]], axis=1)

    def swap_order(state, major, minor):
        flat[0] = state[:, :LANES]
        flat[1] = state[:, LANES:]
        return jnp.concatenate([strided(j, major, minor) for j in range(minor)], axis=0)

    def block_of(level):
        return nq * 2**level if level < low_levels else 2**level

    state = load_state(0)
    for level in range(levels):
        if level == low_levels:
            state = swap_order(state, ns, nq)
        first, second = halves(state, block_of(level))
        paired = jnp.concatenate([first, second], axis=1)
        average = jnp.sum(paired, axis=1, keepdims=True) * (1.0 / (2 * width))
        centered = paired - average * mask
        inverse = lax.rsqrt(jnp.sum(centered * centered, axis=1, keepdims=True) * (1.0 / (2 * width)) + epsilon)
        normed = centered * inverse
        nrm[level] = normed
        inv[level] = inverse
        here = pl.ds(level * pairs, pairs)
        nlc[here, :] = narrow(normed[:, :PAD], normed[:, PAD:], width).astype(BF16)
        preact = row_dot(normed.astype(BF16), wi[...]) + bias
        square = preact * preact
        tangent = jnp.tanh(preact * (tanh_scale + (tanh_scale * cubic_coef) * square))
        half = 0.5 + 0.5 * tangent
        activated = (preact * half).astype(BF16)
        act[here, :] = activated
        slope[level] = half + (0.5 * preact) * (1.0 - tangent * tangent) * (
            tanh_scale + (3.0 * tanh_scale * cubic_coef) * square
        )
        if level + 1 < levels:
            result = gate[0:1] * paired + scale[0:1] * row_dot(activated, wo[...])
            state = unite(result[:, :PAD], result[:, PAD:], block_of(level))

    chunks = gb.shape[0]
    half_chunks = chunks // 2
    span = 2 * width
    units = act.shape[1]
    in_rows, out_rows = span // half_chunks, units // half_chunks
    to_sibling = []

    def start_c(k):
        to_sibling.append(send(gb.at[k, 1 - c], rc.at[k], c_send, c_recv.at[k], sibling))
        to_sibling[k].start()

    plane_waits = []

    def start_d(k):
        to_sibling[k].wait_recv()
        hsum[k] = (gb[k, c].astype(F32) + rc[k].astype(F32)).astype(BF16)
        start, wait = exchange(npl, plane, hsum.at[k], rd.at[k], d_send, d_recv.at[k], id_plane)
        start()
        plane_waits.append(wait)
        rd[k, plane] = hsum[k, plane]

    wait_b1()
    state = swap_order(load_state(1), ns, nq)
    for level in reversed(range(levels)):
        if level == low_levels - 1:
            state = swap_order(state, nq, ns)
        first, second = halves(state, block_of(level))
        upstream = jnp.concatenate([first, second], axis=1)
        branch = scale[0:1] * upstream
        here = pl.ds(level * pairs, pairs)
        bgc[here, :] = narrow(branch[:, :PAD], branch[:, PAD:], width).astype(BF16)
        if level == 0:
            for k in range(half_chunks):
                grad_out = column_dot(act[:, k * out_rows : (k + 1) * out_rows], bgc[...])
                gb[k] = grad_out.reshape(2, npl, 8, span).astype(BF16)
                start_c(k)
        preact_grad = (row_dot(branch.astype(BF16), wot[...]) * slope[level]).astype(BF16)
        pg[here, :] = preact_grad
        if level == 0:
            for k in range(half_chunks):
                start_d(k)
            for k in range(half_chunks):
                grad_in = column_dot(nlc[:, k * in_rows : (k + 1) * in_rows], pg[...])
                for h in range(2):
                    gb[half_chunks + k, h] = grad_in[:, h * span : (h + 1) * span].reshape(npl, 8, span).astype(BF16)
                start_c(half_chunks + k)
        normed_grad = row_dot(preact_grad, wit[...])
        normed = nrm[level]
        mean_grad = jnp.sum(normed_grad, axis=1, keepdims=True) * (1.0 / (2 * width))
        mean_both = jnp.sum(normed_grad * normed, axis=1, keepdims=True) * (1.0 / (2 * width))
        grad = gate[0:1] * upstream + inv[level] * (normed_grad - mean_grad * mask - normed * mean_both)
        state = unite(grad[:, :PAD], grad[:, PAD:], block_of(level))

    tx[...] = state[:, :width].reshape(ns, nq, width).astype(BF16)
    start_u, wait_u = exchange(ns, s, tx, rx1, u_send, u_recv, lambda i: id_qs(q, i))
    start_u()
    rx1[s] = tx[s]

    for k in range(half_chunks, chunks):
        start_d(k)

    def added(ref, count):
        total = ref[0].astype(F32)
        for i in range(1, count):
            total = total + ref[i].astype(F32)
        return total

    z_waits = []
    for k in range(chunks):
        plane_waits[k]()
        rz[k, z] = added(rd.at[k], npl).astype(BF16)
        start, wait = spread(nz, z, rz.at[k], z_send, z_recv.at[k], id_z)
        start()
        z_waits.append(wait)

    wait_u()
    put_rows(rx1[...])
    for j in range(nq):
        tx2[j] = strided(j, ns, nq)[:, :width].astype(BF16)
    start_v, wait_v = exchange(nq, q, tx2, rx2, v_send, v_recv, lambda i: id_qs(i, s))
    start_v()
    rx2[q] = tx2[q]

    gather_waits = []
    for k in range(chunks):
        z_waits[k]()
        rg[k, c, plane] = (added(rz.at[k], nz) * scale_out).astype(BF16)
        start, wait = spread(npl, plane, rg.at[k, c], e_send, e_recv.at[k], id_plane)
        start()
        gather_waits.append(wait)
    over = []

    def put_result(src, dst):
        pltpu.make_async_copy(src, dst, out_sem).start()

    for k in range(chunks):
        gather_waits[k]()
        over.append(send(rg.at[k, c], rg.at[k, c], f_send, f_recv.at[k], sibling))
        over[k].start()
        put_result(rg.at[k, c], grads_out.at[k, c])
    wait_v()
    put_result(rx2, gx_out)
    for k in range(chunks):
        over[k].wait_recv()
        put_result(rg.at[k, 1 - c], grads_out.at[k, 1 - c])

    bytes_of(xs.at[:, pl.ds(0, nq - 1)], a_send).wait()
    bytes_of(tb.at[:, pl.ds(0, ns - 1)], b_send).wait()
    bytes_of(rc, c_send).wait()
    bytes_of(hsum.at[:, pl.ds(0, npl - 1)], d_send).wait()
    bytes_of(rz.at[:, pl.ds(0, nz - 1)], z_send).wait()
    bytes_of(hsum.at[:, pl.ds(0, npl - 1)], e_send).wait()
    bytes_of(rc, f_send).wait()
    bytes_of(tx.at[pl.ds(0, ns - 1)], u_send).wait()
    bytes_of(tx2.at[pl.ds(0, nq - 1)], v_send).wait()
    pltpu.make_async_copy(rx2, gx_out, out_sem).wait()
    pltpu.make_async_copy(rg, grads_out, out_sem).wait()


def finish(gx_ref, out_ref, in_ref, gxt_ref, gin_ref, gout_ref):
    @pl.when(pl.program_id(0) == 0)
    def _():
        rows = gx_ref.shape[0] * gx_ref.shape[1]
        gxt_ref[...] = gx_ref[...].reshape(rows, gx_ref.shape[2]).T

    span = gout_ref.shape[1]
    for h in range(2):
        gin_ref[:, h * span : (h + 1) * span] = in_ref[0, h].astype(F32).reshape(gin_ref.shape[0], span)
    gout_ref[...] = out_ref[0].astype(F32).reshape(gout_ref.shape)


def build(mesh, dims):
    ny, nz, nx, nc = dims
    nq, ns, npl = ny * nz, nx * nc, ny * nx
    rows, pairs = nq * ns, nq * ns // 2
    levels = rows.bit_length() - 1

    def step(saved_input, cotangent, w_in, bias_in, w_out, residual_logit, branch_scale):
        width, units = saved_input.shape[1], w_in.shape[1]
        span = 2 * width
        half_chunks = span // (npl * 8)
        chunks = 2 * half_chunks
        vmem = pltpu.VMEM
        dma = pltpu.SemaphoreType.DMA
        scratch = [
            vmem((2, width, rows), BF16),
            vmem((span, units), BF16),
            vmem((units,), F32),
            vmem((units, span), BF16),
            vmem((span,), F32),
            vmem((span,), F32),
            vmem((2, nq, ns, width), BF16),
            vmem((2, nq, ns, width), BF16),
            vmem((2, ns, nq, width), BF16),
            vmem((2, ns, nq, width), BF16),
            vmem((2, rows, LANES), F32),
            vmem((2 * PAD, units), BF16),
            vmem((units, 2 * PAD), BF16),
            vmem((units, 2 * PAD), BF16),
            vmem((2 * PAD, units), BF16),
            vmem((8, 2 * PAD), F32),
            vmem((8, 2 * PAD), F32),
            vmem((levels, pairs, 2 * PAD), F32),
            vmem((levels, pairs, 1), F32),
            vmem((levels, pairs, units), F32),
            vmem((levels * pairs, span), BF16),
            vmem((levels * pairs, units), BF16),
            vmem((levels * pairs, units), BF16),
            vmem((levels * pairs, span), BF16),
            vmem((chunks, 2, npl, 8, span), BF16),
            vmem((chunks, npl, 8, span), BF16),
            vmem((chunks, npl, 8, span), BF16),
            vmem((chunks, npl, 8, span), BF16),
            vmem((chunks, nz, 8, span), BF16),
            vmem((chunks, 2, npl, 8, span), BF16),
            vmem((ns, nq, width), BF16),
            vmem((ns, nq, width), BF16),
            vmem((nq, ns, width), BF16),
            vmem((nq, ns, width), BF16),
            dma((7,)),
            dma, dma((2,)),
            dma, dma((2,)),
            dma, dma((chunks,)),
            dma, dma((chunks,)),
            dma, dma((chunks,)),
            dma, dma((chunks,)),
            dma, dma((chunks,)),
            dma, dma,
            dma, dma,
            dma,
        ]
        gx, grads = pl.pallas_call(
            functools.partial(kernel, dims, float(rows * rows) ** (-0.5)),
            out_shape=(
                jax.ShapeDtypeStruct((nq, ns, width), BF16),
                jax.ShapeDtypeStruct((chunks, 2, npl, 8, span), BF16),
            ),
            in_specs=[pl.BlockSpec(memory_space=pl.ANY)] * 7,
            out_specs=(pl.BlockSpec(memory_space=pl.ANY),) * 2,
            scratch_shapes=scratch,
            compiler_params=pltpu.CompilerParams(collective_id=0, has_side_effects=True, vmem_limit_bytes=62 * 2**20),
        )(saved_input.T, cotangent.T, w_in, bias_in, w_out, residual_logit, branch_scale)
        gxt, grad_in, grad_out = pl.pallas_call(
            finish,
            grid=(half_chunks,),
            out_shape=(
                jax.ShapeDtypeStruct((width, rows), BF16),
                jax.ShapeDtypeStruct((span, units), F32),
                jax.ShapeDtypeStruct((units, span), F32),
            ),
            in_specs=[
                pl.BlockSpec((nq, ns, width), lambda k: (0, 0, 0)),
                pl.BlockSpec((1, 2, npl, 8, span), lambda k: (k, 0, 0, 0, 0)),
                pl.BlockSpec((1, 2, npl, 8, span), lambda k: (half_chunks + k, 0, 0, 0, 0)),
            ],
            out_specs=(
                pl.BlockSpec((width, rows), lambda k: (0, 0)),
                pl.BlockSpec((span // half_chunks, units), lambda k: (k, 0)),
                pl.BlockSpec((units // half_chunks, span), lambda k: (k, 0)),
            ),
        )(gx, grads, grads)
        return gxt.T, grad_in, grad_out

    in_specs = (P("seq", None), P("seq", None), P(), P(), P(), P(), P())
    out_specs = (P("seq", None), P(), P())
    return jax.shard_map(step, mesh=mesh, in_specs=in_specs, out_specs=out_specs, check_vma=False)


def solution(mesh):
    return build(mesh, (4, 8, 4, 2))
```

```python
import functools

import jax
import jax.numpy as jnp
from jax import lax
from jax.experimental import pallas as pl
from jax.experimental.pallas import tpu as pltpu
from jax.sharding import PartitionSpec as P

epsilon = 1e-05
tanh_scale = 0.7978845608028654
cubic_coef = 0.044715
LANES = 128
PAD = 256
F32 = jnp.float32
BF16 = jnp.bfloat16


def row_dot(left, right):
    return jnp.dot(left, right, preferred_element_type=F32)


def column_dot(left, right):
    return lax.dot_general(left, right, (((0,), (0,)), ((), ())), preferred_element_type=F32)


def lanes_below(rows, lanes, bound):
    return lax.broadcasted_iota(jnp.int32, (rows, lanes), 1) < bound


def widen(values, width):
    rows = values.shape[0]
    keep = lanes_below(rows, PAD, width)
    first = jnp.where(keep, values[:, :PAD], 0.0)
    second = pltpu.roll(values[:, 2 * width - PAD :], width, 1)
    return jnp.concatenate([first, jnp.where(keep, second, 0.0)], axis=1)


def narrow(first, second, width):
    moved = pltpu.roll(second, width - LANES, 1)
    return jnp.concatenate([first[:, :LANES], first[:, LANES:] + moved[:, :LANES], moved[:, LANES:]], axis=1)


def halves(state, block):
    rows = state.shape[0]
    view = state.reshape(rows // (2 * block), 2, block, PAD)
    return view[:, 0].reshape(rows // 2, PAD), view[:, 1].reshape(rows // 2, PAD)


def unite(first, second, block):
    rows = first.shape[0]
    parts = [h.reshape(rows // block, 1, block, PAD) for h in (first, second)]
    return jnp.concatenate(parts, axis=1).reshape(2 * rows, PAD)


def kernel(
    dims, scale_out,
    xt_hbm, ct_hbm, win_hbm, bias_hbm, wout_hbm, logit_hbm, scale_hbm,
    gx_out, grads_out,
    xt, win, bias_row, wout, logit_row, scale_row, xs,
    ra, tb, rb, flat, wi, wit, wo, wot, gate, scale,
    nrm, inv, slope, nlc, act, pg, bgc,
    gb, rc, hsum, rd, rz, rg, tx, rx1, tx2, rx2,
    load_sem, a_send, a_recv, b_send, b_recv, c_send, c_recv, d_send, d_recv, z_send, z_recv,
    e_send, e_recv, f_send, f_recv, u_send, u_recv, v_send, v_recv, out_sem,
):
    ny, nz, nx, nc = dims
    ns, npl = nx * nc, ny * nx
    ng = ny * ns
    rows, pairs = nz * ng, nz * ng // 2
    width = xt.shape[1]
    low_levels, mid_levels = ns.bit_length() - 1, (ns * nz).bit_length() - 1
    levels = rows.bit_length() - 1
    me = lax.axis_index("seq")
    q, s = lax.div(me, ns), lax.rem(me, ns)
    y, z, xc, c = lax.div(q, nz), lax.rem(q, nz), lax.div(s, nc), lax.rem(s, nc)
    plane = y * nx + xc

    group = y * ns + s

    def id_of(zz, gg):
        return (lax.div(gg, ns) * nz + zz) * ns + lax.rem(gg, ns)

    def id_plane(pp):
        return ((lax.div(pp, nx) * nz + z) * nx + lax.rem(pp, nx)) * nc + c

    def id_z(zz):
        return id_of(zz, group)

    def id_group(gg):
        return id_of(z, gg)

    sibling = id_group(group + 1 - 2 * c)

    barrier = pltpu.get_barrier_semaphore()

    def greet(device):
        pl.semaphore_signal(barrier, inc=1, device_id=(device,), device_id_type=pl.DeviceIdType.MESH)

    @pl.loop(1, nz)
    def _(j):
        greet(id_z(lax.rem(z + j, nz)))

    @pl.loop(1, ng)
    def _(j):
        greet(id_group(lax.rem(group + j, ng)))

    operands = (
        (xt_hbm, xt.at[0]), (ct_hbm, xt.at[1]), (logit_hbm, logit_row), (scale_hbm, scale_row), (bias_hbm, bias_row),
        (win_hbm, win), (wout_hbm, wout),
    )
    loads = [pltpu.make_async_copy(src, dst, load_sem.at[i]) for i, (src, dst) in enumerate(operands)]
    for load in loads:
        load.start()
    flat[...] = jnp.zeros_like(flat)
    for k in range(2):
        loads[k].wait()
        xs[k] = xt[k].T.reshape(nz, ng, width)
    for load in loads[2:]:
        load.wait()
    wide_in = jnp.zeros((PAD - width, win.shape[1]), BF16)
    wi[:width] = win[:width]
    wi[width:PAD] = wide_in
    wi[PAD : PAD + width] = win[width:]
    wi[PAD + width :] = wide_in
    wit[...] = wi[...].T
    wo[...] = widen(wout[...].astype(F32), width).astype(BF16)
    wot[...] = wo[...].T
    gate[...] = jax.nn.sigmoid(widen(jnp.broadcast_to(logit_row[...].reshape(1, 2 * width), (8, 2 * width)), width))
    scale[...] = widen(jnp.broadcast_to(scale_row[...].reshape(1, 2 * width), (8, 2 * width)), width)
    bias = bias_row[...].reshape(1, bias_row.shape[0])
    lane = lax.broadcasted_iota(jnp.int32, (1, 2 * PAD), 1) % PAD
    mask = jnp.where(lane < width, 1.0, 0.0)

    pl.semaphore_wait(barrier, (nz - 1) + (ng - 1))

    def send(src, dst, send_sem, recv_sem, device):
        return pltpu.make_async_remote_copy(
            src_ref=src, dst_ref=dst, send_sem=send_sem, recv_sem=recv_sem,
            device_id=(device,), device_id_type=pl.DeviceIdType.MESH,
        )

    def bytes_of(ref, sem):
        return pltpu.make_async_copy(ref, ref, sem)

    def each(count, copy, landing, recv_sem):
        def start():
            @pl.loop(1, count)
            def _(j):
                copy(j).start()

        return start, bytes_of(landing.at[pl.ds(0, count - 1)], recv_sem).wait

    def exchange(count, place, src, dst, send_sem, recv_sem, device_of):
        def copy(j):
            to = lax.rem(place + j, count)
            return send(src.at[to], dst.at[place], send_sem, recv_sem, device_of(to))

        return each(count, copy, dst, recv_sem)

    def spread(count, place, ref, send_sem, recv_sem, device_of):
        def copy(j):
            return send(ref.at[place], ref.at[place], send_sem, recv_sem, device_of(lax.rem(place + j, count)))

        return each(count, copy, ref, recv_sem)

    def start_a(k):
        start, wait = exchange(nz, z, xs.at[k], ra.at[k], a_send, a_recv.at[k], id_z)
        start()
        ra[k, z] = xs[k, z]
        return wait

    def put_rows(block):
        values = block.astype(F32).reshape(rows, width)
        flat[0] = values[:, :LANES]
        flat[1, :, : width - LANES] = values[:, LANES:]

    def strided(start, size, stride):
        return jnp.concatenate([flat[h, pl.ds(start, size, stride=stride), :] for h in range(2)], axis=1)

    def start_b(k):
        put_rows(ra[k])
        for g in range(ng):
            tb[k, g] = strided(g, nz, ng)[:, :width].astype(BF16)
        start, wait = exchange(ng, group, tb.at[k], rb.at[k], b_send, b_recv.at[k], id_group)
        start()
        rb[k, group] = tb[k, group]
        return wait

    wait_a0 = start_a(0)
    wait_a1 = start_a(1)
    wait_a0()
    wait_b0 = start_b(0)
    wait_a1()
    wait_b1 = start_b(1)
    wait_b0()

    def load_state(k):
        put_rows(rb[k])
        return jnp.concatenate([flat[0], flat[1]], axis=1)

    def swap_order(state, major, minor):
        flat[0] = state[:, :LANES]
        flat[1] = state[:, LANES:]
        return jnp.concatenate([strided(j, major, minor) for j in range(minor)], axis=0)

    def block_of(level):
        if level < low_levels:
            return nz * 2**level
        return ng * 2 ** (level - low_levels) if level < mid_levels else ns * 2 ** (level - mid_levels)

    state = load_state(0)
    for level in range(levels):
        if level == low_levels:
            state = swap_order(state, ng, nz)
        first, second = halves(state, block_of(level))
        paired = jnp.concatenate([first, second], axis=1)
        average = jnp.sum(paired, axis=1, keepdims=True) * (1.0 / (2 * width))
        centered = paired - average * mask
        inverse = lax.rsqrt(jnp.sum(centered * centered, axis=1, keepdims=True) * (1.0 / (2 * width)) + epsilon)
        normed = centered * inverse
        nrm[level] = normed
        inv[level] = inverse
        here = pl.ds(level * pairs, pairs)
        nlc[here, :] = narrow(normed[:, :PAD], normed[:, PAD:], width).astype(BF16)
        preact = row_dot(normed.astype(BF16), wi[...]) + bias
        square = preact * preact
        tangent = jnp.tanh(preact * (tanh_scale + (tanh_scale * cubic_coef) * square))
        half = 0.5 + 0.5 * tangent
        product = preact * half
        activated = product.astype(BF16)
        act[here, :] = activated
        slope[level] = half + (product - product * half) * (
            (2.0 * tanh_scale) + (6.0 * tanh_scale * cubic_coef) * square
        )
        if level + 1 < levels:
            result = gate[0:1] * paired + scale[0:1] * row_dot(activated, wo[...])
            state = unite(result[:, :PAD], result[:, PAD:], block_of(level))

    chunks = gb.shape[0]
    half_chunks = chunks // 2
    span = 2 * width
    units = act.shape[1]
    in_rows, out_rows = span // half_chunks, units // half_chunks
    to_sibling = []

    def start_c(k):
        to_sibling.append(send(gb.at[k, 1 - c], rc.at[k], c_send, c_recv.at[k], sibling))
        to_sibling[k].start()

    plane_waits = []

    def start_d(k):
        to_sibling[k].wait_recv()
        hsum[k] = gb[k, c] + rc[k]
        start, wait = exchange(npl, plane, hsum.at[k], rd.at[k], d_send, d_recv.at[k], id_plane)
        start()
        plane_waits.append(wait)
        rd[k, plane] = hsum[k, plane]

    wait_b1()
    state = swap_order(load_state(1), ng, nz)
    for level in reversed(range(levels)):
        if level == low_levels - 1:
            state = swap_order(state, nz, ng)
        first, second = halves(state, block_of(level))
        upstream = jnp.concatenate([first, second], axis=1)
        branch = scale[0:1] * upstream
        here = pl.ds(level * pairs, pairs)
        bgc[here, :] = narrow(branch[:, :PAD], branch[:, PAD:], width).astype(BF16)
        preact_grad = (row_dot(branch.astype(BF16), wot[...]) * slope[level]).astype(BF16)
        pg[here, :] = preact_grad
        if level == 0:
            for k in range(half_chunks):
                grad_out = column_dot(act[:, k * out_rows : (k + 1) * out_rows], bgc[...])
                gb[k] = grad_out.reshape(2, npl, 8, span).astype(BF16)
                start_c(k)
            for k in range(half_chunks):
                grad_in = column_dot(nlc[:, k * in_rows : (k + 1) * in_rows], pg[...])
                for h in range(2):
                    gb[half_chunks + k, h] = grad_in[:, h * span : (h + 1) * span].reshape(npl, 8, span).astype(BF16)
                start_c(half_chunks + k)
            for k in range(chunks):
                start_d(k)
        normed_grad = row_dot(preact_grad, wit[...])
        normed = nrm[level]
        mean_grad = jnp.sum(normed_grad, axis=1, keepdims=True) * (1.0 / (2 * width))
        mean_both = jnp.sum(normed_grad * normed, axis=1, keepdims=True) * (1.0 / (2 * width))
        grad = gate[0:1] * upstream + inv[level] * (normed_grad - mean_grad * mask - normed * mean_both)
        state = unite(grad[:, :PAD], grad[:, PAD:], block_of(level))

    tx[...] = state[:, :width].reshape(ng, nz, width).astype(BF16)
    start_u, wait_u = exchange(ng, group, tx, rx1, u_send, u_recv, id_group)
    start_u()
    rx1[group] = tx[group]

    def added(ref, count):
        total = ref[0].astype(F32)
        for i in range(1, count):
            total = total + ref[i].astype(F32)
        return total

    z_waits = []
    for k in range(chunks):
        plane_waits[k]()
        rz[k, z] = added(rd.at[k], npl).astype(BF16)
        start, wait = spread(nz, z, rz.at[k], z_send, z_recv.at[k], id_z)
        start()
        z_waits.append(wait)

    wait_u()
    put_rows(rx1[...])
    for j in range(nz):
        tx2[j] = strided(j, ng, nz)[:, :width].astype(BF16)
    start_v, wait_v = exchange(nz, z, tx2, rx2, v_send, v_recv, id_z)
    start_v()
    rx2[z] = tx2[z]

    gather_waits = []
    for k in range(chunks):
        z_waits[k]()
        rg[k, c, plane] = (added(rz.at[k], nz) * scale_out).astype(BF16)
        start, wait = spread(npl, plane, rg.at[k, c], e_send, e_recv.at[k], id_plane)
        start()
        gather_waits.append(wait)
    over = []

    def put_result(src, dst):
        pltpu.make_async_copy(src, dst, out_sem).start()

    for k in range(chunks):
        gather_waits[k]()
        over.append(send(rg.at[k, c], rg.at[k, c], f_send, f_recv.at[k], sibling))
        over[k].start()
        put_result(rg.at[k, c], grads_out.at[k, c])
    wait_v()
    put_result(rx2, gx_out)
    for k in range(chunks):
        over[k].wait_recv()
        put_result(rg.at[k, 1 - c], grads_out.at[k, 1 - c])

    bytes_of(xs.at[:, pl.ds(0, nz - 1)], a_send).wait()
    bytes_of(tb.at[:, pl.ds(0, ng - 1)], b_send).wait()
    bytes_of(rc, c_send).wait()
    bytes_of(hsum.at[:, pl.ds(0, npl - 1)], d_send).wait()
    bytes_of(rz.at[:, pl.ds(0, nz - 1)], z_send).wait()
    bytes_of(hsum.at[:, pl.ds(0, npl - 1)], e_send).wait()
    bytes_of(rc, f_send).wait()
    bytes_of(tx.at[pl.ds(0, ng - 1)], u_send).wait()
    bytes_of(tx2.at[pl.ds(0, nz - 1)], v_send).wait()
    pltpu.make_async_copy(rx2, gx_out, out_sem).wait()
    pltpu.make_async_copy(rg, grads_out, out_sem).wait()


def finish(gx_hbm, grads_hbm, gxt_hbm, gin_hbm, gout_hbm, gx, grads, gxt, gin, gout, in_sem, out_sem):
    chunks = grads.shape[0]
    half_chunks = chunks // 2
    span, units = gin.shape
    in_rows, out_rows = span // half_chunks, units // half_chunks
    loads = [pltpu.make_async_copy(grads_hbm.at[k], grads.at[k], in_sem.at[k]) for k in range(chunks)]
    loads.append(pltpu.make_async_copy(gx_hbm, gx, in_sem.at[chunks]))
    for load in loads:
        load.start()
    for k in range(half_chunks):
        loads[k].wait()
        here = pl.ds(k * out_rows, out_rows)
        gout[here, :] = grads[k].astype(F32).reshape(out_rows, span)
        pltpu.make_async_copy(gout.at[here], gout_hbm.at[here], out_sem.at[0]).start()
    for k in range(half_chunks):
        loads[half_chunks + k].wait()
        here = pl.ds(k * in_rows, in_rows)
        for h in range(2):
            gin[here, h * span : (h + 1) * span] = grads[half_chunks + k, h].astype(F32).reshape(in_rows, span)
        pltpu.make_async_copy(gin.at[here], gin_hbm.at[here], out_sem.at[1]).start()
    loads[chunks].wait()
    gxt[...] = gx[...].reshape(gxt.shape[1], gxt.shape[0]).T
    last = pltpu.make_async_copy(gxt, gxt_hbm, out_sem.at[2])
    last.start()
    pltpu.make_async_copy(gout, gout_hbm, out_sem.at[0]).wait()
    pltpu.make_async_copy(gin, gin_hbm, out_sem.at[1]).wait()
    last.wait()


def build(mesh, dims):
    ny, nz, nx, nc = dims
    npl, ng = ny * nx, ny * nx * nc
    rows, pairs = nz * ng, nz * ng // 2
    levels = rows.bit_length() - 1

    def step(saved_input, cotangent, w_in, bias_in, w_out, residual_logit, branch_scale):
        width, units = saved_input.shape[1], w_in.shape[1]
        span = 2 * width
        half_chunks = span // (npl * 8)
        chunks = 2 * half_chunks
        vmem = pltpu.VMEM
        dma = pltpu.SemaphoreType.DMA
        scratch = [
            vmem((2, width, rows), BF16),
            vmem((span, units), BF16),
            vmem((units,), F32),
            vmem((units, span), BF16),
            vmem((span,), F32),
            vmem((span,), F32),
            vmem((2, nz, ng, width), BF16),
            vmem((2, nz, ng, width), BF16),
            vmem((2, ng, nz, width), BF16),
            vmem((2, ng, nz, width), BF16),
            vmem((2, rows, LANES), F32),
            vmem((2 * PAD, units), BF16),
            vmem((units, 2 * PAD), BF16),
            vmem((units, 2 * PAD), BF16),
            vmem((2 * PAD, units), BF16),
            vmem((8, 2 * PAD), F32),
            vmem((8, 2 * PAD), F32),
            vmem((levels, pairs, 2 * PAD), F32),
            vmem((levels, pairs, 1), F32),
            vmem((levels, pairs, units), F32),
            vmem((levels * pairs, span), BF16),
            vmem((levels * pairs, units), BF16),
            vmem((levels * pairs, units), BF16),
            vmem((levels * pairs, span), BF16),
            vmem((chunks, 2, npl, 8, span), BF16),
            vmem((chunks, npl, 8, span), BF16),
            vmem((chunks, npl, 8, span), BF16),
            vmem((chunks, npl, 8, span), BF16),
            vmem((chunks, nz, 8, span), BF16),
            vmem((chunks, 2, npl, 8, span), BF16),
            vmem((ng, nz, width), BF16),
            vmem((ng, nz, width), BF16),
            vmem((nz, ng, width), BF16),
            vmem((nz, ng, width), BF16),
            dma((7,)),
            dma, dma((2,)),
            dma, dma((2,)),
            dma, dma((chunks,)),
            dma, dma((chunks,)),
            dma, dma((chunks,)),
            dma, dma((chunks,)),
            dma, dma((chunks,)),
            dma, dma,
            dma, dma,
            dma,
        ]
        gx, grads = pl.pallas_call(
            functools.partial(kernel, dims, float(rows * rows) ** (-0.5)),
            out_shape=(
                jax.ShapeDtypeStruct((nz, ng, width), BF16),
                jax.ShapeDtypeStruct((chunks, 2, npl, 8, span), BF16),
            ),
            in_specs=[pl.BlockSpec(memory_space=pl.ANY)] * 7,
            out_specs=(pl.BlockSpec(memory_space=pl.ANY),) * 2,
            scratch_shapes=scratch,
            compiler_params=pltpu.CompilerParams(collective_id=0, has_side_effects=True, vmem_limit_bytes=62 * 2**20),
        )(saved_input.T, cotangent.T, w_in, bias_in, w_out, residual_logit, branch_scale)
        gxt, grad_in, grad_out = pl.pallas_call(
            finish,
            out_shape=(
                jax.ShapeDtypeStruct((width, rows), BF16),
                jax.ShapeDtypeStruct((span, units), F32),
                jax.ShapeDtypeStruct((units, span), F32),
            ),
            in_specs=[pl.BlockSpec(memory_space=pl.ANY)] * 2,
            out_specs=(pl.BlockSpec(memory_space=pl.ANY),) * 3,
            scratch_shapes=[
                vmem(gx.shape, BF16), vmem(grads.shape, BF16),
                vmem((width, rows), BF16), vmem((span, units), F32), vmem((units, span), F32),
                dma((chunks + 1,)), dma((3,)),
            ],
            compiler_params=pltpu.CompilerParams(vmem_limit_bytes=62 * 2**20),
        )(gx, grads)
        return gxt.T, grad_in, grad_out

    in_specs = (P("seq", None), P("seq", None), P(), P(), P(), P(), P())
    out_specs = (P("seq", None), P(), P())
    return jax.shard_map(step, mesh=mesh, in_specs=in_specs, out_specs=out_specs, check_vma=False)


def solution(mesh):
    return build(mesh, (4, 8, 4, 2))
```

```python
import functools

import jax
import jax.numpy as jnp
from jax import lax
from jax.experimental import pallas as pl
from jax.experimental.pallas import tpu as pltpu
from jax.sharding import PartitionSpec as P

epsilon = 1e-05
tanh_scale = 0.7978845608028654
cubic_coef = 0.044715
LANES = 128
PAD = 256
F32 = jnp.float32
BF16 = jnp.bfloat16


def row_dot(left, right):
    return jnp.dot(left, right, preferred_element_type=F32)


def column_dot(left, right):
    return lax.dot_general(left, right, (((0,), (0,)), ((), ())), preferred_element_type=F32)


def lanes_below(rows, lanes, bound):
    return lax.broadcasted_iota(jnp.int32, (rows, lanes), 1) < bound


def widen(values, width):
    rows = values.shape[0]
    keep = lanes_below(rows, PAD, width)
    first = jnp.where(keep, values[:, :PAD], 0.0)
    second = pltpu.roll(values[:, 2 * width - PAD :], width, 1)
    return jnp.concatenate([first, jnp.where(keep, second, 0.0)], axis=1)


def narrow(first, second, width):
    moved = pltpu.roll(second, width - LANES, 1)
    return jnp.concatenate([first[:, :LANES], first[:, LANES:] + moved[:, :LANES], moved[:, LANES:]], axis=1)


def halves(state, block):
    rows = state.shape[0]
    view = state.reshape(rows // (2 * block), 2, block, PAD)
    return view[:, 0].reshape(rows // 2, PAD), view[:, 1].reshape(rows // 2, PAD)


def unite(first, second, block):
    rows = first.shape[0]
    parts = [h.reshape(rows // block, 1, block, PAD) for h in (first, second)]
    return jnp.concatenate(parts, axis=1).reshape(2 * rows, PAD)


def kernel(
    dims, scale_out,
    xt_hbm, ct_hbm, win_hbm, bias_hbm, wout_hbm, logit_hbm, scale_hbm,
    gx_out, grads_out,
    xt, win, bias_row, wout, logit_row, scale_row, xs,
    ra, tb, rb, flat, wi, wit, wo, wot, gate, scale,
    nrm, inv, slope, nlc, act, pg, bgc,
    gb, rc, hsum, rd, rz, rg, tx, rx1, tx2, rx2,
    load_sem, a_send, a_recv, b_send, b_recv, c_send, c_recv, d_send, d_recv, z_send, z_recv,
    e_send, e_recv, f_send, f_recv, u_send, u_recv, v_send, v_recv, out_sem,
):
    ny, nz, nx, nc = dims
    ns, npl = nx * nc, ny * nx
    ng = ny * ns
    rows, pairs = nz * ng, nz * ng // 2
    width = xt.shape[1]
    low_levels, mid_levels = ns.bit_length() - 1, (ns * nz).bit_length() - 1
    levels = rows.bit_length() - 1
    me = lax.axis_index("seq")
    q, s = lax.div(me, ns), lax.rem(me, ns)
    y, z, xc, c = lax.div(q, nz), lax.rem(q, nz), lax.div(s, nc), lax.rem(s, nc)
    plane = y * nx + xc

    group = y * ns + s

    def id_of(zz, gg):
        return (lax.div(gg, ns) * nz + zz) * ns + lax.rem(gg, ns)

    def id_plane(pp):
        return ((lax.div(pp, nx) * nz + z) * nx + lax.rem(pp, nx)) * nc + c

    def id_z(zz):
        return id_of(zz, group)

    def id_group(gg):
        return id_of(z, gg)

    sibling = id_group(group + 1 - 2 * c)

    barrier = pltpu.get_barrier_semaphore()

    def greet(device):
        pl.semaphore_signal(barrier, inc=1, device_id=(device,), device_id_type=pl.DeviceIdType.MESH)

    @pl.loop(1, nz)
    def _(j):
        greet(id_z(lax.rem(z + j, nz)))

    @pl.loop(1, ng)
    def _(j):
        greet(id_group(lax.rem(group + j, ng)))

    operands = (
        (xt_hbm, xt.at[0]), (ct_hbm, xt.at[1]), (logit_hbm, logit_row), (scale_hbm, scale_row), (bias_hbm, bias_row),
        (win_hbm, win), (wout_hbm, wout),
    )
    loads = [pltpu.make_async_copy(src, dst, load_sem.at[i]) for i, (src, dst) in enumerate(operands)]
    for load in loads:
        load.start()
    flat[...] = jnp.zeros_like(flat)
    def put_rows(block):
        values = block.astype(F32).reshape(rows, width)
        flat[0] = values[:, :LANES]
        flat[1, :, : width - LANES] = values[:, LANES:]

    def fold():
        tails = flat[1].reshape(nz, 2, ng // 2, LANES)
        moved = pltpu.roll(tails[:, 1].reshape(rows // 2, LANES), width - LANES, 1)
        both = tails[:, 0] + moved.reshape(nz, ng // 2, LANES)
        return jnp.concatenate([flat[0].reshape(nz, ng, LANES), both], axis=1).astype(BF16)

    def unfold(block):
        both = block[:, ng:].astype(F32)
        moved = pltpu.roll(both.reshape(rows // 2, LANES), 2 * LANES - width, 1).reshape(nz, ng // 2, LANES)
        flat[0] = block[:, :ng].astype(F32).reshape(rows, LANES)
        flat[1, :, : width - LANES] = jnp.concatenate([both, moved], axis=1).reshape(rows, LANES)[:, : width - LANES]

    for k in range(2):
        loads[k].wait()
        put_rows(xt[k].T)
        xs[k] = fold()
    for load in loads[2:]:
        load.wait()
    wide_in = jnp.zeros((PAD - width, win.shape[1]), BF16)
    wi[:width] = win[:width]
    wi[width:PAD] = wide_in
    wi[PAD : PAD + width] = win[width:]
    wi[PAD + width :] = wide_in
    wit[...] = wi[...].T
    wo[...] = widen(wout[...].astype(F32), width).astype(BF16)
    wot[...] = wo[...].T
    gate[...] = jax.nn.sigmoid(widen(jnp.broadcast_to(logit_row[...].reshape(1, 2 * width), (8, 2 * width)), width))
    scale[...] = widen(jnp.broadcast_to(scale_row[...].reshape(1, 2 * width), (8, 2 * width)), width)
    bias = bias_row[...].reshape(1, bias_row.shape[0])
    lane = lax.broadcasted_iota(jnp.int32, (1, 2 * PAD), 1) % PAD
    mask = jnp.where(lane < width, 1.0, 0.0)

    pl.semaphore_wait(barrier, (nz - 1) + (ng - 1))

    def send(src, dst, send_sem, recv_sem, device):
        return pltpu.make_async_remote_copy(
            src_ref=src, dst_ref=dst, send_sem=send_sem, recv_sem=recv_sem,
            device_id=(device,), device_id_type=pl.DeviceIdType.MESH,
        )

    def bytes_of(ref, sem):
        return pltpu.make_async_copy(ref, ref, sem)

    def each(count, copy, landing, recv_sem):
        def start():
            @pl.loop(1, count)
            def _(j):
                copy(j).start()

        return start, bytes_of(landing.at[pl.ds(0, count - 1)], recv_sem).wait

    def exchange(count, place, src, dst, send_sem, recv_sem, device_of):
        def copy(j):
            to = lax.rem(place + j, count)
            return send(src.at[to], dst.at[place], send_sem, recv_sem, device_of(to))

        return each(count, copy, dst, recv_sem)

    def spread(count, place, ref, send_sem, recv_sem, device_of):
        def copy(j):
            return send(ref.at[place], ref.at[place], send_sem, recv_sem, device_of(lax.rem(place + j, count)))

        return each(count, copy, ref, recv_sem)

    def start_a(k):
        start, wait = exchange(nz, z, xs.at[k], ra.at[k], a_send, a_recv.at[k], id_z)
        start()
        ra[k, z] = xs[k, z]
        return wait

    def strided(start, size, stride):
        return jnp.concatenate([flat[h, pl.ds(start, size, stride=stride), :] for h in range(2)], axis=1)

    def start_b(k):
        unfold(ra[k])
        for g in range(ng):
            tb[k, g] = strided(g, nz, ng)[:, :width].astype(BF16)
        start, wait = exchange(ng, group, tb.at[k], rb.at[k], b_send, b_recv.at[k], id_group)
        start()
        rb[k, group] = tb[k, group]
        return wait

    wait_a0 = start_a(0)
    wait_a1 = start_a(1)
    wait_a0()
    wait_b0 = start_b(0)
    wait_a1()
    wait_b1 = start_b(1)
    wait_b0()

    def load_state(k):
        put_rows(rb[k])
        return jnp.concatenate([flat[0], flat[1]], axis=1)

    def swap_order(state, major, minor):
        flat[0] = state[:, :LANES]
        flat[1] = state[:, LANES:]
        return jnp.concatenate([strided(j, major, minor) for j in range(minor)], axis=0)

    def block_of(level):
        if level < low_levels:
            return nz * 2**level
        return ng * 2 ** (level - low_levels) if level < mid_levels else ns * 2 ** (level - mid_levels)

    state = load_state(0)
    for level in range(levels):
        if level == low_levels:
            state = swap_order(state, ng, nz)
        first, second = halves(state, block_of(level))
        paired = jnp.concatenate([first, second], axis=1)
        average = jnp.sum(paired, axis=1, keepdims=True) * (1.0 / (2 * width))
        centered = paired - average * mask
        inverse = lax.rsqrt(jnp.sum(centered * centered, axis=1, keepdims=True) * (1.0 / (2 * width)) + epsilon)
        normed = centered * inverse
        nrm[level] = normed
        inv[level] = inverse
        here = pl.ds(level * pairs, pairs)
        nlc[here, :] = narrow(normed[:, :PAD], normed[:, PAD:], width).astype(BF16)
        preact = row_dot(normed.astype(BF16), wi[...]) + bias
        square = preact * preact
        tangent = jnp.tanh(preact * (tanh_scale + (tanh_scale * cubic_coef) * square))
        half = 0.5 + 0.5 * tangent
        product = preact * half
        activated = product.astype(BF16)
        act[here, :] = activated
        slope[level] = half + (product - product * half) * (
            (2.0 * tanh_scale) + (6.0 * tanh_scale * cubic_coef) * square
        )
        if level + 1 < levels:
            result = gate[0:1] * paired + scale[0:1] * row_dot(activated, wo[...])
            state = unite(result[:, :PAD], result[:, PAD:], block_of(level))

    chunks = gb.shape[0]
    half_chunks = chunks // 2
    span = 2 * width
    units = act.shape[1]
    in_rows, out_rows = span // half_chunks, units // half_chunks
    to_sibling = []

    def start_c(k):
        to_sibling.append(send(gb.at[k, 1 - c], rc.at[k], c_send, c_recv.at[k], sibling))
        to_sibling[k].start()

    plane_waits = []

    def start_d(k):
        to_sibling[k].wait_recv()
        hsum[k] = gb[k, c] + rc[k]
        start, wait = exchange(npl, plane, hsum.at[k], rd.at[k], d_send, d_recv.at[k], id_plane)
        start()
        plane_waits.append(wait)
        rd[k, plane] = hsum[k, plane]

    wait_b1()
    state = swap_order(load_state(1), ng, nz)
    for level in reversed(range(levels)):
        if level == low_levels - 1:
            state = swap_order(state, nz, ng)
        first, second = halves(state, block_of(level))
        upstream = jnp.concatenate([first, second], axis=1)
        branch = scale[0:1] * upstream
        here = pl.ds(level * pairs, pairs)
        bgc[here, :] = narrow(branch[:, :PAD], branch[:, PAD:], width).astype(BF16)
        if level == 0:
            grad_out = column_dot(act[...], bgc[...])
            for k in range(half_chunks):
                gb[k] = grad_out[k * out_rows : (k + 1) * out_rows].reshape(2, npl, 8, span).astype(BF16)
                start_c(k)
        preact_grad = (row_dot(branch.astype(BF16), wot[...]) * slope[level]).astype(BF16)
        pg[here, :] = preact_grad
        if level == 0:
            for k in range(half_chunks):
                start_d(k)
            grad_in = column_dot(nlc[...], pg[...])
            for k in range(half_chunks):
                for h in range(2):
                    part = grad_in[k * in_rows : (k + 1) * in_rows, h * span : (h + 1) * span]
                    gb[half_chunks + k, h] = part.reshape(npl, 8, span).astype(BF16)
                start_c(half_chunks + k)
        normed_grad = row_dot(preact_grad, wit[...])
        normed = nrm[level]
        mean_grad = jnp.sum(normed_grad, axis=1, keepdims=True) * (1.0 / (2 * width))
        mean_both = jnp.sum(normed_grad * normed, axis=1, keepdims=True) * (1.0 / (2 * width))
        grad = gate[0:1] * upstream + inv[level] * (normed_grad - mean_grad * mask - normed * mean_both)
        state = unite(grad[:, :PAD], grad[:, PAD:], block_of(level))

    tx[...] = state[:, :width].reshape(ng, nz, width).astype(BF16)
    start_u, wait_u = exchange(ng, group, tx, rx1, u_send, u_recv, id_group)
    start_u()
    for k in range(half_chunks, chunks):
        start_d(k)
    rx1[group] = tx[group]

    def added(ref, count):
        total = ref[0].astype(F32)
        for i in range(1, count):
            total = total + ref[i].astype(F32)
        return total

    z_waits = []
    for k in range(chunks):
        plane_waits[k]()
        rz[k, z] = added(rd.at[k], npl).astype(BF16)
        start, wait = spread(nz, z, rz.at[k], z_send, z_recv.at[k], id_z)
        start()
        z_waits.append(wait)

    def return_rows():
        wait_u()
        put_rows(rx1[...])
        for j in range(nz):
            tx2[j] = strided(j, ng, nz)[:, :width].astype(BF16)
        start_v, wait_v = exchange(nz, z, tx2, rx2, v_send, v_recv, id_z)
        start_v()
        rx2[z] = tx2[z]
        return wait_v

    gather_waits = []
    for k in range(chunks):
        z_waits[k]()
        rg[k, c, plane] = (added(rz.at[k], nz) * scale_out).astype(BF16)
        start, wait = spread(npl, plane, rg.at[k, c], e_send, e_recv.at[k], id_plane)
        start()
        gather_waits.append(wait)
        if k == half_chunks:
            wait_v = return_rows()
    over = []

    def put_result(src, dst):
        pltpu.make_async_copy(src, dst, out_sem).start()

    for k in range(chunks):
        gather_waits[k]()
        over.append(send(rg.at[k, c], rg.at[k, c], f_send, f_recv.at[k], sibling))
        over[k].start()
        put_result(rg.at[k, c], grads_out.at[k, c])
    wait_v()
    put_result(rx2, gx_out)
    for k in range(chunks):
        over[k].wait_recv()
        put_result(rg.at[k, 1 - c], grads_out.at[k, 1 - c])

    bytes_of(xs.at[:, pl.ds(0, nz - 1)], a_send).wait()
    bytes_of(tb.at[:, pl.ds(0, ng - 1)], b_send).wait()
    bytes_of(rc, c_send).wait()
    bytes_of(hsum.at[:, pl.ds(0, npl - 1)], d_send).wait()
    bytes_of(rz.at[:, pl.ds(0, nz - 1)], z_send).wait()
    bytes_of(hsum.at[:, pl.ds(0, npl - 1)], e_send).wait()
    bytes_of(rc, f_send).wait()
    bytes_of(tx.at[pl.ds(0, ng - 1)], u_send).wait()
    bytes_of(tx2.at[pl.ds(0, nz - 1)], v_send).wait()
    pltpu.make_async_copy(rx2, gx_out, out_sem).wait()
    pltpu.make_async_copy(rg, grads_out, out_sem).wait()


def finish(gx_hbm, grads_hbm, gxt_hbm, gin_hbm, gout_hbm, gx, grads, gxt, gin, gout, in_sem, out_sem):
    chunks = grads.shape[0]
    half_chunks = chunks // 2
    span, units = gin.shape
    in_rows, out_rows = span // half_chunks, units // half_chunks
    loads = [pltpu.make_async_copy(grads_hbm.at[k], grads.at[k], in_sem.at[k]) for k in range(chunks)]
    loads.append(pltpu.make_async_copy(gx_hbm, gx, in_sem.at[chunks]))
    for load in loads:
        load.start()
    for k in range(half_chunks):
        loads[k].wait()
        here = pl.ds(k * out_rows, out_rows)
        gout[here, :] = grads[k].astype(F32).reshape(out_rows, span)
        pltpu.make_async_copy(gout.at[here], gout_hbm.at[here], out_sem.at[0]).start()
    for k in range(half_chunks):
        loads[half_chunks + k].wait()
        here = pl.ds(k * in_rows, in_rows)
        for h in range(2):
            gin[here, h * span : (h + 1) * span] = grads[half_chunks + k, h].astype(F32).reshape(in_rows, span)
        pltpu.make_async_copy(gin.at[here], gin_hbm.at[here], out_sem.at[1]).start()
    loads[chunks].wait()
    gxt[...] = gx[...].reshape(gxt.shape[1], gxt.shape[0]).T
    last = pltpu.make_async_copy(gxt, gxt_hbm, out_sem.at[2])
    last.start()
    pltpu.make_async_copy(gout, gout_hbm, out_sem.at[0]).wait()
    pltpu.make_async_copy(gin, gin_hbm, out_sem.at[1]).wait()
    last.wait()


def build(mesh, dims):
    ny, nz, nx, nc = dims
    npl, ng = ny * nx, ny * nx * nc
    rows, pairs = nz * ng, nz * ng // 2
    levels = rows.bit_length() - 1

    def step(saved_input, cotangent, w_in, bias_in, w_out, residual_logit, branch_scale):
        width, units = saved_input.shape[1], w_in.shape[1]
        span = 2 * width
        half_chunks = span // (npl * 8)
        chunks = 2 * half_chunks
        vmem = pltpu.VMEM
        dma = pltpu.SemaphoreType.DMA
        scratch = [
            vmem((2, width, rows), BF16),
            vmem((span, units), BF16),
            vmem((units,), F32),
            vmem((units, span), BF16),
            vmem((span,), F32),
            vmem((span,), F32),
            vmem((2, nz, ng + ng // 2, LANES), BF16),
            vmem((2, nz, ng + ng // 2, LANES), BF16),
            vmem((2, ng, nz, width), BF16),
            vmem((2, ng, nz, width), BF16),
            vmem((2, rows, LANES), F32),
            vmem((2 * PAD, units), BF16),
            vmem((units, 2 * PAD), BF16),
            vmem((units, 2 * PAD), BF16),
            vmem((2 * PAD, units), BF16),
            vmem((8, 2 * PAD), F32),
            vmem((8, 2 * PAD), F32),
            vmem((levels, pairs, 2 * PAD), F32),
            vmem((levels, pairs, 1), F32),
            vmem((levels, pairs, units), F32),
            vmem((levels * pairs, span), BF16),
            vmem((levels * pairs, units), BF16),
            vmem((levels * pairs, units), BF16),
            vmem((levels * pairs, span), BF16),
            vmem((chunks, 2, npl, 8, span), BF16),
            vmem((chunks, npl, 8, span), BF16),
            vmem((chunks, npl, 8, span), BF16),
            vmem((chunks, npl, 8, span), BF16),
            vmem((chunks, nz, 8, span), BF16),
            vmem((chunks, 2, npl, 8, span), BF16),
            vmem((ng, nz, width), BF16),
            vmem((ng, nz, width), BF16),
            vmem((nz, ng, width), BF16),
            vmem((nz, ng, width), BF16),
            dma((7,)),
            dma, dma((2,)),
            dma, dma((2,)),
            dma, dma((chunks,)),
            dma, dma((chunks,)),
            dma, dma((chunks,)),
            dma, dma((chunks,)),
            dma, dma((chunks,)),
            dma, dma,
            dma, dma,
            dma,
        ]
        gx, grads = pl.pallas_call(
            functools.partial(kernel, dims, float(rows * rows) ** (-0.5)),
            out_shape=(
                jax.ShapeDtypeStruct((nz, ng, width), BF16),
                jax.ShapeDtypeStruct((chunks, 2, npl, 8, span), BF16),
            ),
            in_specs=[pl.BlockSpec(memory_space=pl.ANY)] * 7,
            out_specs=(pl.BlockSpec(memory_space=pl.ANY),) * 2,
            scratch_shapes=scratch,
            compiler_params=pltpu.CompilerParams(collective_id=0, has_side_effects=True, vmem_limit_bytes=62 * 2**20),
        )(saved_input.T, cotangent.T, w_in, bias_in, w_out, residual_logit, branch_scale)
        gxt, grad_in, grad_out = pl.pallas_call(
            finish,
            out_shape=(
                jax.ShapeDtypeStruct((width, rows), BF16),
                jax.ShapeDtypeStruct((span, units), F32),
                jax.ShapeDtypeStruct((units, span), F32),
            ),
            in_specs=[pl.BlockSpec(memory_space=pl.ANY)] * 2,
            out_specs=(pl.BlockSpec(memory_space=pl.ANY),) * 3,
            scratch_shapes=[
                vmem(gx.shape, BF16), vmem(grads.shape, BF16),
                vmem((width, rows), BF16), vmem((span, units), F32), vmem((units, span), F32),
                dma((chunks + 1,)), dma((3,)),
            ],
            compiler_params=pltpu.CompilerParams(vmem_limit_bytes=62 * 2**20),
        )(gx, grads)
        return gxt.T, grad_in, grad_out

    in_specs = (P("seq", None), P("seq", None), P(), P(), P(), P(), P())
    out_specs = (P("seq", None), P(), P())
    return jax.shard_map(step, mesh=mesh, in_specs=in_specs, out_specs=out_specs, check_vma=False)


def solution(mesh):
    return build(mesh, (4, 8, 4, 2))
```

```python
import functools

import jax
import jax.numpy as jnp
from jax import lax
from jax.experimental import pallas as pl
from jax.experimental.pallas import tpu as pltpu
from jax.sharding import PartitionSpec as P

epsilon = 1e-05
tanh_scale = 0.7978845608028654
cubic_coef = 0.044715
LANES = 128
PAD = 256
F32 = jnp.float32
BF16 = jnp.bfloat16


def row_dot(left, right):
    return jnp.dot(left, right, preferred_element_type=F32)


def column_dot(left, right):
    return lax.dot_general(left, right, (((0,), (0,)), ((), ())), preferred_element_type=F32)


def lanes_below(rows, lanes, bound):
    return lax.broadcasted_iota(jnp.int32, (rows, lanes), 1) < bound


def widen(values, width):
    rows = values.shape[0]
    keep = lanes_below(rows, PAD, width)
    first = jnp.where(keep, values[:, :PAD], 0.0)
    second = pltpu.roll(values[:, 2 * width - PAD :], width, 1)
    return jnp.concatenate([first, jnp.where(keep, second, 0.0)], axis=1)


def narrow(first, second, width):
    moved = pltpu.roll(second, width - LANES, 1)
    return jnp.concatenate([first[:, :LANES], first[:, LANES:] + moved[:, :LANES], moved[:, LANES:]], axis=1)


def halves(state, block):
    rows = state.shape[0]
    view = state.reshape(rows // (2 * block), 2, block, PAD)
    return view[:, 0].reshape(rows // 2, PAD), view[:, 1].reshape(rows // 2, PAD)


def unite(first, second, block):
    rows = first.shape[0]
    parts = [h.reshape(rows // block, 1, block, PAD) for h in (first, second)]
    return jnp.concatenate(parts, axis=1).reshape(2 * rows, PAD)


def kernel(
    dims, scale_out,
    xt_hbm, ct_hbm, win_hbm, bias_hbm, wout_hbm, logit_hbm, scale_hbm,
    rx2, rg,
    xt, win, bias_row, wout, logit_row, scale_row, xs,
    ra, tb, rb, flat, wi, wit, wo, wot, gate, scale,
    nrm, inv, slope, nlc, act, pg, bgc,
    gb, rc, hsum, rd, rz, tx, rx1, tx2,
    load_sem, a_send, a_recv, b_send, b_recv, c_send, c_recv, d_send, d_recv, z_send, z_recv,
    e_send, e_recv, f_send, f_recv, u_send, u_recv, v_send, v_recv,
):
    ny, nz, nx, nc = dims
    ns, npl = nx * nc, ny * nx
    ng = ny * ns
    rows, pairs = nz * ng, nz * ng // 2
    width = xt.shape[1]
    low_levels, mid_levels = ns.bit_length() - 1, (ns * nz).bit_length() - 1
    levels = rows.bit_length() - 1
    me = lax.axis_index("seq")
    q, s = lax.div(me, ns), lax.rem(me, ns)
    y, z, xc, c = lax.div(q, nz), lax.rem(q, nz), lax.div(s, nc), lax.rem(s, nc)
    plane = y * nx + xc

    group = y * ns + s

    def id_of(zz, gg):
        return (lax.div(gg, ns) * nz + zz) * ns + lax.rem(gg, ns)

    def id_plane(pp):
        return ((lax.div(pp, nx) * nz + z) * nx + lax.rem(pp, nx)) * nc + c

    def id_z(zz):
        return id_of(zz, group)

    def id_group(gg):
        return id_of(z, gg)

    sibling = id_group(group + 1 - 2 * c)

    barrier = pltpu.get_barrier_semaphore()

    def greet(device):
        pl.semaphore_signal(barrier, inc=1, device_id=(device,), device_id_type=pl.DeviceIdType.MESH)

    @pl.loop(1, nz)
    def _(j):
        greet(id_z(lax.rem(z + j, nz)))

    @pl.loop(1, ng)
    def _(j):
        greet(id_group(lax.rem(group + j, ng)))

    operands = (
        (xt_hbm, xt.at[0]), (ct_hbm, xt.at[1]), (logit_hbm, logit_row), (scale_hbm, scale_row), (bias_hbm, bias_row),
        (win_hbm, win), (wout_hbm, wout),
    )
    loads = [pltpu.make_async_copy(src, dst, load_sem.at[i]) for i, (src, dst) in enumerate(operands)]
    for load in loads:
        load.start()
    flat[...] = jnp.zeros_like(flat)
    def put_rows(block):
        values = block.astype(F32).reshape(rows, width)
        flat[0] = values[:, :LANES]
        flat[1, :, : width - LANES] = values[:, LANES:]

    def fold():
        tails = flat[1].reshape(nz, 2, ng // 2, LANES)
        moved = pltpu.roll(tails[:, 1].reshape(rows // 2, LANES), width - LANES, 1)
        both = tails[:, 0] + moved.reshape(nz, ng // 2, LANES)
        return jnp.concatenate([flat[0].reshape(nz, ng, LANES), both], axis=1).astype(BF16)

    def unfold(block):
        both = block[:, ng:].astype(F32)
        moved = pltpu.roll(both.reshape(rows // 2, LANES), 2 * LANES - width, 1).reshape(nz, ng // 2, LANES)
        flat[0] = block[:, :ng].astype(F32).reshape(rows, LANES)
        flat[1, :, : width - LANES] = jnp.concatenate([both, moved], axis=1).reshape(rows, LANES)[:, : width - LANES]

    for k in range(2):
        loads[k].wait()
        put_rows(xt[k].T)
        xs[k] = fold()
    for load in loads[2:]:
        load.wait()
    wide_in = jnp.zeros((PAD - width, win.shape[1]), BF16)
    wi[:width] = win[:width]
    wi[width:PAD] = wide_in
    wi[PAD : PAD + width] = win[width:]
    wi[PAD + width :] = wide_in
    wit[...] = wi[...].T
    wo[...] = widen(wout[...].astype(F32), width).astype(BF16)
    wot[...] = wo[...].T
    gate[...] = jax.nn.sigmoid(widen(jnp.broadcast_to(logit_row[...].reshape(1, 2 * width), (8, 2 * width)), width))
    scale[...] = widen(jnp.broadcast_to(scale_row[...].reshape(1, 2 * width), (8, 2 * width)), width)
    bias = bias_row[...].reshape(1, bias_row.shape[0])
    lane = lax.broadcasted_iota(jnp.int32, (1, 2 * PAD), 1) % PAD
    mask = jnp.where(lane < width, 1.0, 0.0)

    pl.semaphore_wait(barrier, (nz - 1) + (ng - 1))

    def send(src, dst, send_sem, recv_sem, device):
        return pltpu.make_async_remote_copy(
            src_ref=src, dst_ref=dst, send_sem=send_sem, recv_sem=recv_sem,
            device_id=(device,), device_id_type=pl.DeviceIdType.MESH,
        )

    def bytes_of(ref, sem):
        return pltpu.make_async_copy(ref, ref, sem)

    def each(count, copy, landing, recv_sem):
        def start():
            @pl.loop(1, count)
            def _(j):
                copy(j).start()

        return start, bytes_of(landing.at[pl.ds(0, count - 1)], recv_sem).wait

    def exchange(count, place, src, dst, send_sem, recv_sem, device_of):
        def copy(j):
            to = lax.rem(place + j, count)
            return send(src.at[to], dst.at[place], send_sem, recv_sem, device_of(to))

        return each(count, copy, dst, recv_sem)

    def spread(count, place, ref, send_sem, recv_sem, device_of):
        def copy(j):
            return send(ref.at[place], ref.at[place], send_sem, recv_sem, device_of(lax.rem(place + j, count)))

        return each(count, copy, ref, recv_sem)

    def start_a(k):
        start, wait = exchange(nz, z, xs.at[k], ra.at[k], a_send, a_recv.at[k], id_z)
        start()
        ra[k, z] = xs[k, z]
        return wait

    def strided(start, size, stride):
        return jnp.concatenate([flat[h, pl.ds(start, size, stride=stride), :] for h in range(2)], axis=1)

    def start_b(k):
        unfold(ra[k])
        for g in range(ng):
            tb[k, g] = strided(g, nz, ng)[:, :width].astype(BF16)
        start, wait = exchange(ng, group, tb.at[k], rb.at[k], b_send, b_recv.at[k], id_group)
        start()
        rb[k, group] = tb[k, group]
        return wait

    wait_a0 = start_a(0)
    wait_a1 = start_a(1)
    wait_a0()
    wait_b0 = start_b(0)
    wait_a1()
    wait_b1 = start_b(1)
    wait_b0()

    def load_state(k):
        put_rows(rb[k])
        return jnp.concatenate([flat[0], flat[1]], axis=1)

    def swap_order(state, major, minor):
        flat[0] = state[:, :LANES]
        flat[1] = state[:, LANES:]
        return jnp.concatenate([strided(j, major, minor) for j in range(minor)], axis=0)

    def block_of(level):
        if level < low_levels:
            return nz * 2**level
        return ng * 2 ** (level - low_levels) if level < mid_levels else ns * 2 ** (level - mid_levels)

    state = load_state(0)
    for level in range(levels):
        if level == low_levels:
            state = swap_order(state, ng, nz)
        first, second = halves(state, block_of(level))
        paired = jnp.concatenate([first, second], axis=1)
        average = jnp.sum(paired, axis=1, keepdims=True) * (1.0 / (2 * width))
        centered = paired - average * mask
        inverse = lax.rsqrt(jnp.sum(centered * centered, axis=1, keepdims=True) * (1.0 / (2 * width)) + epsilon)
        normed = centered * inverse
        nrm[level] = normed
        inv[level] = inverse
        here = pl.ds(level * pairs, pairs)
        nlc[here, :] = narrow(normed[:, :PAD], normed[:, PAD:], width).astype(BF16)
        preact = row_dot(normed.astype(BF16), wi[...]) + bias
        square = preact * preact
        tangent = jnp.tanh(preact * (tanh_scale + (tanh_scale * cubic_coef) * square))
        half = 0.5 + 0.5 * tangent
        product = preact * half
        activated = product.astype(BF16)
        act[here, :] = activated
        slope[level] = half + (product - product * half) * (
            (2.0 * tanh_scale) + (6.0 * tanh_scale * cubic_coef) * square
        )
        if level + 1 < levels:
            result = gate[0:1] * paired + scale[0:1] * row_dot(activated, wo[...])
            state = unite(result[:, :PAD], result[:, PAD:], block_of(level))

    chunks = gb.shape[0]
    half_chunks = chunks // 2
    span = 2 * width
    units = act.shape[1]
    in_rows, out_rows = span // half_chunks, units // half_chunks
    to_sibling = []

    def start_c(k):
        to_sibling.append(send(gb.at[k, 1 - c], rc.at[k], c_send, c_recv.at[k], sibling))
        to_sibling[k].start()

    plane_waits = []

    def start_d(k):
        to_sibling[k].wait_recv()
        hsum[k] = gb[k, c] + rc[k]
        start, wait = exchange(npl, plane, hsum.at[k], rd.at[k], d_send, d_recv.at[k], id_plane)
        start()
        plane_waits.append(wait)
        rd[k, plane] = hsum[k, plane]

    wait_b1()
    state = swap_order(load_state(1), ng, nz)
    for level in reversed(range(levels)):
        if level == low_levels - 1:
            state = swap_order(state, nz, ng)
        first, second = halves(state, block_of(level))
        upstream = jnp.concatenate([first, second], axis=1)
        branch = scale[0:1] * upstream
        here = pl.ds(level * pairs, pairs)
        bgc[here, :] = narrow(branch[:, :PAD], branch[:, PAD:], width).astype(BF16)
        if level == 0:
            grad_out = column_dot(act[...], bgc[...])
            for k in range(half_chunks):
                gb[k] = grad_out[k * out_rows : (k + 1) * out_rows].reshape(2, npl, 8, span).astype(BF16)
                start_c(k)
        preact_grad = (row_dot(branch.astype(BF16), wot[...]) * slope[level]).astype(BF16)
        pg[here, :] = preact_grad
        if level == 0:
            for k in range(half_chunks):
                start_d(k)
            grad_in = column_dot(nlc[...], pg[...])
            for k in range(half_chunks):
                for h in range(2):
                    part = grad_in[k * in_rows : (k + 1) * in_rows, h * span : (h + 1) * span]
                    gb[half_chunks + k, h] = part.reshape(npl, 8, span).astype(BF16)
                start_c(half_chunks + k)
        normed_grad = row_dot(preact_grad, wit[...])
        normed = nrm[level]
        mean_grad = jnp.sum(normed_grad, axis=1, keepdims=True) * (1.0 / (2 * width))
        mean_both = jnp.sum(normed_grad * normed, axis=1, keepdims=True) * (1.0 / (2 * width))
        grad = gate[0:1] * upstream + inv[level] * (normed_grad - mean_grad * mask - normed * mean_both)
        state = unite(grad[:, :PAD], grad[:, PAD:], block_of(level))

    tx[...] = state[:, :width].reshape(ng, nz, width).astype(BF16)
    start_u, wait_u = exchange(ng, group, tx, rx1, u_send, u_recv, id_group)
    for k in range(half_chunks, chunks):
        start_d(k)
    start_u()
    rx1[group] = tx[group]

    def added(ref, count):
        total = ref[0].astype(F32)
        for i in range(1, count):
            total = total + ref[i].astype(F32)
        return total

    z_waits = []
    for k in range(chunks):
        plane_waits[k]()
        rz[k, z] = added(rd.at[k], npl).astype(BF16)
        start, wait = spread(nz, z, rz.at[k], z_send, z_recv.at[k], id_z)
        start()
        z_waits.append(wait)

    def return_rows():
        wait_u()
        put_rows(rx1[...])
        for j in range(nz):
            tx2[j] = strided(j, ng, nz)[:, :width].astype(BF16)
        start_v, wait_v = exchange(nz, z, tx2, rx2, v_send, v_recv, id_z)
        start_v()
        rx2[z] = tx2[z]
        return wait_v

    gather_waits = []
    for k in range(chunks):
        z_waits[k]()
        rg[k, c, plane] = (added(rz.at[k], nz) * scale_out).astype(BF16)
        start, wait = spread(npl, plane, rg.at[k, c], e_send, e_recv.at[k], id_plane)
        start()
        gather_waits.append(wait)
        if k == chunks - 2:
            wait_v = return_rows()
    over = []

    for k in range(chunks):
        gather_waits[k]()
        over.append(send(rg.at[k, c], rg.at[k, c], f_send, f_recv.at[k], sibling))
        over[k].start()
    wait_v()
    for k in range(chunks):
        over[k].wait_recv()

    bytes_of(xs.at[:, pl.ds(0, nz - 1)], a_send).wait()
    bytes_of(tb.at[:, pl.ds(0, ng - 1)], b_send).wait()
    bytes_of(rc, c_send).wait()
    bytes_of(hsum.at[:, pl.ds(0, npl - 1)], d_send).wait()
    bytes_of(rz.at[:, pl.ds(0, nz - 1)], z_send).wait()
    bytes_of(hsum.at[:, pl.ds(0, npl - 1)], e_send).wait()
    bytes_of(rc, f_send).wait()
    bytes_of(tx.at[pl.ds(0, ng - 1)], u_send).wait()
    bytes_of(tx2.at[pl.ds(0, nz - 1)], v_send).wait()


def finish(gx, grads, gxt_hbm, gin_hbm, gout_hbm, gxt, gin, gout, out_sem):
    half_chunks = grads.shape[0] // 2
    span, units = gin.shape
    in_rows, out_rows = span // half_chunks, units // half_chunks
    for k in range(half_chunks):
        here = pl.ds(k * out_rows, out_rows)
        gout[here, :] = grads[k].astype(F32).reshape(out_rows, span)
        pltpu.make_async_copy(gout.at[here], gout_hbm.at[here], out_sem.at[0]).start()
    for k in range(half_chunks):
        here = pl.ds(k * in_rows, in_rows)
        for h in range(2):
            gin[here, h * span : (h + 1) * span] = grads[half_chunks + k, h].astype(F32).reshape(in_rows, span)
        pltpu.make_async_copy(gin.at[here], gin_hbm.at[here], out_sem.at[1]).start()
    gxt[...] = gx[...].reshape(gxt.shape[1], gxt.shape[0]).T
    last = pltpu.make_async_copy(gxt, gxt_hbm, out_sem.at[2])
    last.start()
    pltpu.make_async_copy(gout, gout_hbm, out_sem.at[0]).wait()
    pltpu.make_async_copy(gin, gin_hbm, out_sem.at[1]).wait()
    last.wait()


def build(mesh, dims):
    ny, nz, nx, nc = dims
    npl, ng = ny * nx, ny * nx * nc
    rows, pairs = nz * ng, nz * ng // 2
    levels = rows.bit_length() - 1

    def step(saved_input, cotangent, w_in, bias_in, w_out, residual_logit, branch_scale):
        width, units = saved_input.shape[1], w_in.shape[1]
        span = 2 * width
        half_chunks = span // (npl * 8)
        chunks = 2 * half_chunks
        vmem = pltpu.VMEM
        dma = pltpu.SemaphoreType.DMA
        scratch = [
            vmem((2, width, rows), BF16),
            vmem((span, units), BF16),
            vmem((units,), F32),
            vmem((units, span), BF16),
            vmem((span,), F32),
            vmem((span,), F32),
            vmem((2, nz, ng + ng // 2, LANES), BF16),
            vmem((2, nz, ng + ng // 2, LANES), BF16),
            vmem((2, ng, nz, width), BF16),
            vmem((2, ng, nz, width), BF16),
            vmem((2, rows, LANES), F32),
            vmem((2 * PAD, units), BF16),
            vmem((units, 2 * PAD), BF16),
            vmem((units, 2 * PAD), BF16),
            vmem((2 * PAD, units), BF16),
            vmem((8, 2 * PAD), F32),
            vmem((8, 2 * PAD), F32),
            vmem((levels, pairs, 2 * PAD), F32),
            vmem((levels, pairs, 1), F32),
            vmem((levels, pairs, units), F32),
            vmem((levels * pairs, span), BF16),
            vmem((levels * pairs, units), BF16),
            vmem((levels * pairs, units), BF16),
            vmem((levels * pairs, span), BF16),
            vmem((chunks, 2, npl, 8, span), BF16),
            vmem((chunks, npl, 8, span), BF16),
            vmem((chunks, npl, 8, span), BF16),
            vmem((chunks, npl, 8, span), BF16),
            vmem((chunks, nz, 8, span), BF16),
            vmem((ng, nz, width), BF16),
            vmem((ng, nz, width), BF16),
            vmem((nz, ng, width), BF16),
            dma((7,)),
            dma, dma((2,)),
            dma, dma((2,)),
            dma, dma((chunks,)),
            dma, dma((chunks,)),
            dma, dma((chunks,)),
            dma, dma((chunks,)),
            dma, dma((chunks,)),
            dma, dma,
            dma, dma,
        ]
        in_vmem = pl.BlockSpec(memory_space=pltpu.VMEM)
        gx, grads = pl.pallas_call(
            functools.partial(kernel, dims, float(rows * rows) ** (-0.5)),
            out_shape=(vmem((nz, ng, width), BF16), vmem((chunks, 2, npl, 8, span), BF16)),
            in_specs=[pl.BlockSpec(memory_space=pl.ANY)] * 7,
            out_specs=(in_vmem, in_vmem),
            scratch_shapes=scratch,
            compiler_params=pltpu.CompilerParams(collective_id=0, has_side_effects=True, vmem_limit_bytes=60 * 2**20),
        )(saved_input.T, cotangent.T, w_in, bias_in, w_out, residual_logit, branch_scale)
        gxt, grad_in, grad_out = pl.pallas_call(
            finish,
            out_shape=(
                jax.ShapeDtypeStruct((width, rows), BF16),
                jax.ShapeDtypeStruct((span, units), F32),
                jax.ShapeDtypeStruct((units, span), F32),
            ),
            in_specs=[in_vmem] * 2,
            out_specs=(pl.BlockSpec(memory_space=pl.ANY),) * 3,
            scratch_shapes=[
                vmem((width, rows), BF16), vmem((span, units), F32), vmem((units, span), F32), dma((3,)),
            ],
            compiler_params=pltpu.CompilerParams(vmem_limit_bytes=48 * 2**20),
        )(gx, grads)
        return gxt.T, grad_in, grad_out

    in_specs = (P("seq", None), P("seq", None), P(), P(), P(), P(), P())
    out_specs = (P("seq", None), P(), P())
    return jax.shard_map(step, mesh=mesh, in_specs=in_specs, out_specs=out_specs, check_vma=False)


def solution(mesh):
    return build(mesh, (4, 8, 4, 2))
```

```python
import functools

import jax
import jax.numpy as jnp
from jax import lax
from jax.experimental import pallas as pl
from jax.experimental.pallas import tpu as pltpu
from jax.sharding import PartitionSpec as P

epsilon = 1e-05
tanh_scale = 0.7978845608028654
cubic_coef = 0.044715
LANES = 128
PAD = 256
F32 = jnp.float32
BF16 = jnp.bfloat16


def row_dot(left, right):
    return jnp.dot(left, right, preferred_element_type=F32)


def column_dot(left, right):
    return lax.dot_general(left, right, (((0,), (0,)), ((), ())), preferred_element_type=F32)


def lanes_below(rows, lanes, bound):
    return lax.broadcasted_iota(jnp.int32, (rows, lanes), 1) < bound


def widen(values, width):
    rows = values.shape[0]
    keep = lanes_below(rows, PAD, width)
    first = jnp.where(keep, values[:, :PAD], 0.0)
    second = pltpu.roll(values[:, 2 * width - PAD :], width, 1)
    return jnp.concatenate([first, jnp.where(keep, second, 0.0)], axis=1)


def narrow(first, second, width):
    moved = pltpu.roll(second, width - LANES, 1)
    return jnp.concatenate([first[:, :LANES], first[:, LANES:] + moved[:, :LANES], moved[:, LANES:]], axis=1)


def halves(state, block):
    rows = state.shape[0]
    view = state.reshape(rows // (2 * block), 2, block, PAD)
    return view[:, 0].reshape(rows // 2, PAD), view[:, 1].reshape(rows // 2, PAD)


def unite(first, second, block):
    rows = first.shape[0]
    parts = [h.reshape(rows // block, 1, block, PAD) for h in (first, second)]
    return jnp.concatenate(parts, axis=1).reshape(2 * rows, PAD)


def kernel(
    dims, scale_out,
    xt_hbm, ct_hbm, win_hbm, bias_hbm, wout_hbm, logit_hbm, scale_hbm,
    rx2, rg,
    xt, win, bias_row, wout, logit_row, scale_row, xs,
    ra, tb, rb, flat, wi, wit, wo, wot, gate, scale,
    nrm, inv, slope, nlc, act, pg, bgc,
    gb, rc, hsum, rd, rz, tx, rx1, tx2,
    load_sem, a_send, a_recv, b_send, b_recv, c_send, c_recv, d_send, d_recv, z_send, z_recv,
    e_send, e_recv, f_send, f_recv, u_send, u_recv, v_send, v_recv,
):
    ny, nz, nx, nc = dims
    ns, npl = nx * nc, ny * nx
    ng = ny * ns
    rows, pairs = nz * ng, nz * ng // 2
    width = xt.shape[1]
    low_levels, mid_levels = ns.bit_length() - 1, (ns * nz).bit_length() - 1
    levels = rows.bit_length() - 1
    me = lax.axis_index("seq")
    q, s = lax.div(me, ns), lax.rem(me, ns)
    y, z, xc, c = lax.div(q, nz), lax.rem(q, nz), lax.div(s, nc), lax.rem(s, nc)
    plane = y * nx + xc

    group = y * ns + s

    def id_of(zz, gg):
        return (lax.div(gg, ns) * nz + zz) * ns + lax.rem(gg, ns)

    def id_plane(pp):
        return ((lax.div(pp, nx) * nz + z) * nx + lax.rem(pp, nx)) * nc + c

    def id_z(zz):
        return id_of(zz, group)

    def id_group(gg):
        return id_of(z, gg)

    sibling = id_group(group + 1 - 2 * c)

    barrier = pltpu.get_barrier_semaphore()

    def greet(device):
        pl.semaphore_signal(barrier, inc=1, device_id=(device,), device_id_type=pl.DeviceIdType.MESH)

    def hops(step, size):
        return min(step, size - step)

    z_steps = sorted(range(1, nz), key=lambda j: -hops(j, nz))
    group_steps = [(jy, jx, jc) for jy in range(ny) for jx in range(nx) for jc in range(nc)][1:]
    group_steps.sort(key=lambda j: -(hops(j[0], ny) + hops(j[1], nx)))
    at_y, at_z, at_x, at_c = (
        [lax.rem(here + j, size) if j else here for j in range(size)] for here, size in ((y, ny), (z, nz), (xc, nx), (c, nc))
    )
    id_y, id_x = [i * (nz * ns) for i in at_y], [i * nc for i in at_x]
    group_y, own_z, own_group = [i * ns for i in at_y], z * ns, y * (nz * ns) + s
    z_targets = [(at_z[j], at_z[j] * ns + own_group) for j in z_steps]
    group_targets = []
    for jy, jx, jc in group_steps:
        in_plane = id_x[jx] + at_c[jc]
        group_targets.append((group_y[jy] + in_plane, id_y[jy] + own_z + in_plane))
    for _, device in z_targets + group_targets:
        greet(device)

    operands = (
        (xt_hbm, xt.at[0]), (ct_hbm, xt.at[1]), (logit_hbm, logit_row), (scale_hbm, scale_row), (bias_hbm, bias_row),
        (win_hbm, win), (wout_hbm, wout),
    )
    loads = [pltpu.make_async_copy(src, dst, load_sem.at[i]) for i, (src, dst) in enumerate(operands)]
    for load in loads:
        load.start()
    flat[...] = jnp.zeros_like(flat)
    def put_rows(block):
        values = block.astype(F32).reshape(rows, width)
        flat[0] = values[:, :LANES]
        flat[1, :, : width - LANES] = values[:, LANES:]

    def fold():
        tails = flat[1].reshape(nz, 2, ng // 2, LANES)
        moved = pltpu.roll(tails[:, 1].reshape(rows // 2, LANES), width - LANES, 1)
        both = tails[:, 0] + moved.reshape(nz, ng // 2, LANES)
        return jnp.concatenate([flat[0].reshape(nz, ng, LANES), both], axis=1).astype(BF16)

    def unfold(block):
        both = block[:, ng:].astype(F32)
        moved = pltpu.roll(both.reshape(rows // 2, LANES), 2 * LANES - width, 1).reshape(nz, ng // 2, LANES)
        flat[0] = block[:, :ng].astype(F32).reshape(rows, LANES)
        flat[1, :, : width - LANES] = jnp.concatenate([both, moved], axis=1).reshape(rows, LANES)[:, : width - LANES]

    for k in range(2):
        loads[k].wait()
        put_rows(xt[k].T)
        xs[k] = fold()
    for load in loads[2:]:
        load.wait()
    wide_in = jnp.zeros((PAD - width, win.shape[1]), BF16)
    wi[:width] = win[:width]
    wi[width:PAD] = wide_in
    wi[PAD : PAD + width] = win[width:]
    wi[PAD + width :] = wide_in
    wit[...] = wi[...].T
    wo[...] = widen(wout[...].astype(F32), width).astype(BF16)
    wot[...] = wo[...].T
    gate[...] = jax.nn.sigmoid(widen(jnp.broadcast_to(logit_row[...].reshape(1, 2 * width), (8, 2 * width)), width))
    scale[...] = widen(jnp.broadcast_to(scale_row[...].reshape(1, 2 * width), (8, 2 * width)), width)
    bias = bias_row[...].reshape(1, bias_row.shape[0])
    lane = lax.broadcasted_iota(jnp.int32, (1, 2 * PAD), 1) % PAD
    mask = jnp.where(lane < width, 1.0, 0.0)

    pl.semaphore_wait(barrier, (nz - 1) + (ng - 1))

    def send(src, dst, send_sem, recv_sem, device):
        return pltpu.make_async_remote_copy(
            src_ref=src, dst_ref=dst, send_sem=send_sem, recv_sem=recv_sem,
            device_id=(device,), device_id_type=pl.DeviceIdType.MESH,
        )

    def bytes_of(ref, sem):
        return pltpu.make_async_copy(ref, ref, sem)

    def each(count, copy, landing, recv_sem):
        def start():
            @pl.loop(1, count)
            def _(j):
                copy(j).start()

        return start, bytes_of(landing.at[pl.ds(0, count - 1)], recv_sem).wait

    def exchange(count, place, src, dst, send_sem, recv_sem, device_of):
        def copy(j):
            to = lax.rem(place + j, count)
            return send(src.at[to], dst.at[place], send_sem, recv_sem, device_of(to))

        return each(count, copy, dst, recv_sem)

    def spread(count, place, ref, send_sem, recv_sem, device_of):
        def copy(j):
            return send(ref.at[place], ref.at[place], send_sem, recv_sem, device_of(lax.rem(place + j, count)))

        return each(count, copy, ref, recv_sem)

    def exchange_with(targets, place, src, dst, send_sem, recv_sem):
        def start():
            for to, device in targets:
                send(src.at[to], dst.at[place], send_sem, recv_sem, device).start()

        return start, bytes_of(dst.at[pl.ds(0, len(targets))], recv_sem).wait

    def start_a(k):
        start, wait = exchange_with(z_targets, z, xs.at[k], ra.at[k], a_send, a_recv.at[k])
        start()
        ra[k, z] = xs[k, z]
        return wait

    def strided(start, size, stride):
        return jnp.concatenate([flat[h, pl.ds(start, size, stride=stride), :] for h in range(2)], axis=1)

    def start_b(k):
        unfold(ra[k])
        for g in range(ng):
            tb[k, g] = strided(g, nz, ng)[:, :width].astype(BF16)
        start, wait = exchange_with(group_targets, group, tb.at[k], rb.at[k], b_send, b_recv.at[k])
        start()
        rb[k, group] = tb[k, group]
        return wait

    wait_a0 = start_a(0)
    wait_a1 = start_a(1)
    wait_a0()
    wait_b0 = start_b(0)
    wait_a1()
    wait_b1 = start_b(1)
    wait_b0()

    def load_state(k):
        put_rows(rb[k])
        return jnp.concatenate([flat[0], flat[1]], axis=1)

    def swap_order(state, major, minor):
        flat[0] = state[:, :LANES]
        flat[1] = state[:, LANES:]
        return jnp.concatenate([strided(j, major, minor) for j in range(minor)], axis=0)

    def block_of(level):
        if level < low_levels:
            return nz * 2**level
        return ng * 2 ** (level - low_levels) if level < mid_levels else ns * 2 ** (level - mid_levels)

    state = load_state(0)
    for level in range(levels):
        if level == low_levels:
            state = swap_order(state, ng, nz)
        first, second = halves(state, block_of(level))
        paired = jnp.concatenate([first, second], axis=1)
        average = jnp.sum(paired, axis=1, keepdims=True) * (1.0 / (2 * width))
        centered = paired - average * mask
        inverse = lax.rsqrt(jnp.sum(centered * centered, axis=1, keepdims=True) * (1.0 / (2 * width)) + epsilon)
        normed = centered * inverse
        nrm[level] = normed
        inv[level] = inverse
        here = pl.ds(level * pairs, pairs)
        nlc[here, :] = narrow(normed[:, :PAD], normed[:, PAD:], width).astype(BF16)
        preact = row_dot(normed.astype(BF16), wi[...]) + bias
        square = preact * preact
        tangent = jnp.tanh(preact * (tanh_scale + (tanh_scale * cubic_coef) * square))
        half = 0.5 + 0.5 * tangent
        product = preact * half
        activated = product.astype(BF16)
        act[here, :] = activated
        slope[level] = half + (product - product * half) * (
            (2.0 * tanh_scale) + (6.0 * tanh_scale * cubic_coef) * square
        )
        if level + 1 < levels:
            result = gate[0:1] * paired + scale[0:1] * row_dot(activated, wo[...])
            state = unite(result[:, :PAD], result[:, PAD:], block_of(level))

    chunks = gb.shape[0]
    half_chunks = chunks // 2
    span = 2 * width
    units = act.shape[1]
    in_rows, out_rows = span // half_chunks, units // half_chunks
    to_sibling = []

    def start_c(k):
        to_sibling.append(send(gb.at[k, 1 - c], rc.at[k], c_send, c_recv.at[k], sibling))
        to_sibling[k].start()

    plane_waits = []

    def start_d(k):
        to_sibling[k].wait_recv()
        hsum[k] = gb[k, c] + rc[k]
        start, wait = exchange(npl, plane, hsum.at[k], rd.at[k], d_send, d_recv.at[k], id_plane)
        start()
        plane_waits.append(wait)
        rd[k, plane] = hsum[k, plane]

    wait_b1()
    state = swap_order(load_state(1), ng, nz)
    for level in reversed(range(levels)):
        if level == low_levels - 1:
            state = swap_order(state, nz, ng)
        first, second = halves(state, block_of(level))
        upstream = jnp.concatenate([first, second], axis=1)
        branch = scale[0:1] * upstream
        here = pl.ds(level * pairs, pairs)
        bgc[here, :] = narrow(branch[:, :PAD], branch[:, PAD:], width).astype(BF16)
        if level == 0:
            grad_out = column_dot(act[...], bgc[...])
            for k in range(half_chunks):
                gb[k] = grad_out[k * out_rows : (k + 1) * out_rows].reshape(2, npl, 8, span).astype(BF16)
                start_c(k)
        preact_grad = (row_dot(branch.astype(BF16), wot[...]) * slope[level]).astype(BF16)
        pg[here, :] = preact_grad
        if level == 0:
            for k in range(half_chunks):
                start_d(k)
            grad_in = column_dot(nlc[...], pg[...])
            for k in range(half_chunks):
                for h in range(2):
                    part = grad_in[k * in_rows : (k + 1) * in_rows, h * span : (h + 1) * span]
                    gb[half_chunks + k, h] = part.reshape(npl, 8, span).astype(BF16)
                start_c(half_chunks + k)
        normed_grad = row_dot(preact_grad, wit[...])
        normed = nrm[level]
        mean_grad = jnp.sum(normed_grad, axis=1, keepdims=True) * (1.0 / (2 * width))
        mean_both = jnp.sum(normed_grad * normed, axis=1, keepdims=True) * (1.0 / (2 * width))
        grad = gate[0:1] * upstream + inv[level] * (normed_grad - mean_grad * mask - normed * mean_both)
        state = unite(grad[:, :PAD], grad[:, PAD:], block_of(level))

    tx[...] = state[:, :width].reshape(ng, nz, width).astype(BF16)
    start_u, wait_u = exchange(ng, group, tx, rx1, u_send, u_recv, id_group)
    for k in range(half_chunks, chunks):
        start_d(k)
    start_u()
    rx1[group] = tx[group]

    def added(ref, count):
        total = ref[0].astype(F32)
        for i in range(1, count):
            total = total + ref[i].astype(F32)
        return total

    z_waits = []
    for k in range(chunks):
        plane_waits[k]()
        rz[k, z] = added(rd.at[k], npl).astype(BF16)
        start, wait = spread(nz, z, rz.at[k], z_send, z_recv.at[k], id_z)
        start()
        z_waits.append(wait)

    def return_rows():
        wait_u()
        put_rows(rx1[...])
        for j in range(nz):
            tx2[j] = strided(j, ng, nz)[:, :width].astype(BF16)
        start_v, wait_v = exchange(nz, z, tx2, rx2, v_send, v_recv, id_z)
        start_v()
        rx2[z] = tx2[z]
        return wait_v

    gather_waits = []
    for k in range(chunks):
        z_waits[k]()
        rg[k, c, plane] = (added(rz.at[k], nz) * scale_out).astype(BF16)
        start, wait = spread(npl, plane, rg.at[k, c], e_send, e_recv.at[k], id_plane)
        start()
        gather_waits.append(wait)
        if k == chunks - 2:
            wait_v = return_rows()
    over = []

    for k in range(chunks):
        gather_waits[k]()
        over.append(send(rg.at[k, c], rg.at[k, c], f_send, f_recv.at[k], sibling))
        over[k].start()
    wait_v()
    for k in range(chunks):
        over[k].wait_recv()

    bytes_of(xs.at[:, pl.ds(0, nz - 1)], a_send).wait()
    bytes_of(tb.at[:, pl.ds(0, ng - 1)], b_send).wait()
    bytes_of(rc, c_send).wait()
    bytes_of(hsum.at[:, pl.ds(0, npl - 1)], d_send).wait()
    bytes_of(rz.at[:, pl.ds(0, nz - 1)], z_send).wait()
    bytes_of(hsum.at[:, pl.ds(0, npl - 1)], e_send).wait()
    bytes_of(rc, f_send).wait()
    bytes_of(tx.at[pl.ds(0, ng - 1)], u_send).wait()
    bytes_of(tx2.at[pl.ds(0, nz - 1)], v_send).wait()


def finish(gx, grads, gxt_hbm, gin_hbm, gout_hbm, gxt, gin, gout, out_sem):
    half_chunks = grads.shape[0] // 2
    span, units = gin.shape
    in_rows, out_rows = span // half_chunks, units // half_chunks
    for k in range(half_chunks):
        here = pl.ds(k * out_rows, out_rows)
        gout[here, :] = grads[k].astype(F32).reshape(out_rows, span)
        pltpu.make_async_copy(gout.at[here], gout_hbm.at[here], out_sem.at[0]).start()
    for k in range(half_chunks):
        here = pl.ds(k * in_rows, in_rows)
        for h in range(2):
            gin[here, h * span : (h + 1) * span] = grads[half_chunks + k, h].astype(F32).reshape(in_rows, span)
        pltpu.make_async_copy(gin.at[here], gin_hbm.at[here], out_sem.at[1]).start()
    gxt[...] = gx[...].reshape(gxt.shape[1], gxt.shape[0]).T
    last = pltpu.make_async_copy(gxt, gxt_hbm, out_sem.at[2])
    last.start()
    pltpu.make_async_copy(gout, gout_hbm, out_sem.at[0]).wait()
    pltpu.make_async_copy(gin, gin_hbm, out_sem.at[1]).wait()
    last.wait()


def build(mesh, dims):
    ny, nz, nx, nc = dims
    npl, ng = ny * nx, ny * nx * nc
    rows, pairs = nz * ng, nz * ng // 2
    levels = rows.bit_length() - 1

    def step(saved_input, cotangent, w_in, bias_in, w_out, residual_logit, branch_scale):
        width, units = saved_input.shape[1], w_in.shape[1]
        span = 2 * width
        half_chunks = span // (npl * 8)
        chunks = 2 * half_chunks
        vmem = pltpu.VMEM
        dma = pltpu.SemaphoreType.DMA
        scratch = [
            vmem((2, width, rows), BF16),
            vmem((span, units), BF16),
            vmem((units,), F32),
            vmem((units, span), BF16),
            vmem((span,), F32),
            vmem((span,), F32),
            vmem((2, nz, ng + ng // 2, LANES), BF16),
            vmem((2, nz, ng + ng // 2, LANES), BF16),
            vmem((2, ng, nz, width), BF16),
            vmem((2, ng, nz, width), BF16),
            vmem((2, rows, LANES), F32),
            vmem((2 * PAD, units), BF16),
            vmem((units, 2 * PAD), BF16),
            vmem((units, 2 * PAD), BF16),
            vmem((2 * PAD, units), BF16),
            vmem((8, 2 * PAD), F32),
            vmem((8, 2 * PAD), F32),
            vmem((levels, pairs, 2 * PAD), F32),
            vmem((levels, pairs, 1), F32),
            vmem((levels, pairs, units), F32),
            vmem((levels * pairs, span), BF16),
            vmem((levels * pairs, units), BF16),
            vmem((levels * pairs, units), BF16),
            vmem((levels * pairs, span), BF16),
            vmem((chunks, 2, npl, 8, span), BF16),
            vmem((chunks, npl, 8, span), BF16),
            vmem((chunks, npl, 8, span), BF16),
            vmem((chunks, npl, 8, span), BF16),
            vmem((chunks, nz, 8, span), BF16),
            vmem((ng, nz, width), BF16),
            vmem((ng, nz, width), BF16),
            vmem((nz, ng, width), BF16),
            dma((7,)),
            dma, dma((2,)),
            dma, dma((2,)),
            dma, dma((chunks,)),
            dma, dma((chunks,)),
            dma, dma((chunks,)),
            dma, dma((chunks,)),
            dma, dma((chunks,)),
            dma, dma,
            dma, dma,
        ]
        in_vmem = pl.BlockSpec(memory_space=pltpu.VMEM)
        gx, grads = pl.pallas_call(
            functools.partial(kernel, dims, float(rows * rows) ** (-0.5)),
            out_shape=(vmem((nz, ng, width), BF16), vmem((chunks, 2, npl, 8, span), BF16)),
            in_specs=[pl.BlockSpec(memory_space=pl.ANY)] * 7,
            out_specs=(in_vmem, in_vmem),
            scratch_shapes=scratch,
            compiler_params=pltpu.CompilerParams(collective_id=0, has_side_effects=True, vmem_limit_bytes=60 * 2**20),
        )(saved_input.T, cotangent.T, w_in, bias_in, w_out, residual_logit, branch_scale)
        gxt, grad_in, grad_out = pl.pallas_call(
            finish,
            out_shape=(
                jax.ShapeDtypeStruct((width, rows), BF16),
                jax.ShapeDtypeStruct((span, units), F32),
                jax.ShapeDtypeStruct((units, span), F32),
            ),
            in_specs=[in_vmem] * 2,
            out_specs=(pl.BlockSpec(memory_space=pl.ANY),) * 3,
            scratch_shapes=[
                vmem((width, rows), BF16), vmem((span, units), F32), vmem((units, span), F32), dma((3,)),
            ],
            compiler_params=pltpu.CompilerParams(vmem_limit_bytes=48 * 2**20),
        )(gx, grads)
        return gxt.T, grad_in, grad_out

    in_specs = (P("seq", None), P("seq", None), P(), P(), P(), P(), P())
    out_specs = (P("seq", None), P(), P())
    return jax.shard_map(step, mesh=mesh, in_specs=in_specs, out_specs=out_specs, check_vma=False)


def solution(mesh):
    return build(mesh, (4, 8, 4, 2))
```

```python
import functools

import jax
import jax.numpy as jnp
from jax import lax
from jax.experimental import pallas as pl
from jax.experimental.pallas import tpu as pltpu
from jax.sharding import PartitionSpec as P

epsilon = 1e-05
tanh_scale = 0.7978845608028654
cubic_coef = 0.044715
LANES = 128
PAD = 256
F32 = jnp.float32
BF16 = jnp.bfloat16


def row_dot(left, right):
    return jnp.dot(left, right, preferred_element_type=F32)


def column_dot(left, right):
    return lax.dot_general(left, right, (((0,), (0,)), ((), ())), preferred_element_type=F32)


def lanes_below(rows, lanes, bound):
    return lax.broadcasted_iota(jnp.int32, (rows, lanes), 1) < bound


def widen(values, width):
    rows = values.shape[0]
    keep = lanes_below(rows, PAD, width)
    first = jnp.where(keep, values[:, :PAD], 0.0)
    second = pltpu.roll(values[:, 2 * width - PAD :], width, 1)
    return jnp.concatenate([first, jnp.where(keep, second, 0.0)], axis=1)


def narrow(first, second, width):
    moved = pltpu.roll(second, width - LANES, 1)
    return jnp.concatenate([first[:, :LANES], first[:, LANES:] + moved[:, :LANES], moved[:, LANES:]], axis=1)


def halves(state, block):
    rows = state.shape[0]
    view = state.reshape(rows // (2 * block), 2, block, PAD)
    return view[:, 0].reshape(rows // 2, PAD), view[:, 1].reshape(rows // 2, PAD)


def unite(first, second, block):
    rows = first.shape[0]
    parts = [h.reshape(rows // block, 1, block, PAD) for h in (first, second)]
    return jnp.concatenate(parts, axis=1).reshape(2 * rows, PAD)


def kernel(
    dims, scale_out,
    xt_hbm, ct_hbm, win_hbm, bias_hbm, wout_hbm, logit_hbm, scale_hbm,
    rx2, rg,
    xt, win, bias_row, wout, logit_row, scale_row, xs,
    ra, tb, rb, flat, wi, wit, wo, wot, gate, scale,
    nrm, inv, slope, nlc, act, pg, bgc,
    gb, rc, hsum, rd, rz, tx, rx1, tx2,
    load_sem, a_send, a_recv, b_send, b_recv, c_send, c_recv, d_send, d_recv, z_send, z_recv,
    e_send, e_recv, f_send, f_recv, u_send, u_recv, v_send, v_recv,
):
    ny, nz, nx, nc = dims
    ns, npl = nx * nc, ny * nx
    ng = ny * ns
    rows, pairs = nz * ng, nz * ng // 2
    width = xt.shape[1]
    low_levels, mid_levels = ns.bit_length() - 1, (ns * nz).bit_length() - 1
    levels = rows.bit_length() - 1
    me = lax.axis_index("seq")
    q, s = lax.div(me, ns), lax.rem(me, ns)
    y, z, xc, c = lax.div(q, nz), lax.rem(q, nz), lax.div(s, nc), lax.rem(s, nc)
    plane = y * nx + xc

    group = y * ns + s

    def id_of(zz, gg):
        return (lax.div(gg, ns) * nz + zz) * ns + lax.rem(gg, ns)

    def id_z(zz):
        return id_of(zz, group)

    def id_group(gg):
        return id_of(z, gg)

    sibling = id_group(group + 1 - 2 * c)

    barrier = pltpu.get_barrier_semaphore()

    def greet(device):
        pl.semaphore_signal(barrier, inc=1, device_id=(device,), device_id_type=pl.DeviceIdType.MESH)

    def hops(step, size):
        return min(step, size - step)

    z_steps = sorted(range(1, nz), key=lambda j: -hops(j, nz))
    group_steps = [(jy, jx, jc) for jy in range(ny) for jx in range(nx) for jc in range(nc)][1:]
    group_steps.sort(key=lambda j: -(hops(j[0], ny) + hops(j[1], nx)))
    at_y, at_z, at_x, at_c = (
        [lax.rem(here + j, size) if j else here for j in range(size)] for here, size in ((y, ny), (z, nz), (xc, nx), (c, nc))
    )
    id_y, id_x = [i * (nz * ns) for i in at_y], [i * nc for i in at_x]
    group_y, own_z, own_group = [i * ns for i in at_y], z * ns, y * (nz * ns) + s
    z_targets = [(at_z[j], at_z[j] * ns + own_group) for j in z_steps]
    group_targets = []
    for jy, jx, jc in group_steps:
        in_plane = id_x[jx] + at_c[jc]
        group_targets.append((group_y[jy] + in_plane, id_y[jy] + own_z + in_plane))
    plane_y = [i * nx for i in at_y]
    plane_targets = [
        (plane_y[jy] + at_x[jx], id_y[jy] + own_z + id_x[jx] + c) for jy, jx, jc in group_steps if jc == 0
    ]
    for _, device in z_targets + group_targets:
        greet(device)

    operands = (
        (xt_hbm, xt.at[0]), (ct_hbm, xt.at[1]), (logit_hbm, logit_row), (scale_hbm, scale_row), (bias_hbm, bias_row),
        (win_hbm, win), (wout_hbm, wout),
    )
    loads = [pltpu.make_async_copy(src, dst, load_sem.at[i]) for i, (src, dst) in enumerate(operands)]
    for load in loads:
        load.start()
    flat[...] = jnp.zeros_like(flat)
    def put_rows(block):
        values = block.astype(F32).reshape(rows, width)
        flat[0] = values[:, :LANES]
        flat[1, :, : width - LANES] = values[:, LANES:]

    def fold():
        tails = flat[1].reshape(nz, 2, ng // 2, LANES)
        moved = pltpu.roll(tails[:, 1].reshape(rows // 2, LANES), width - LANES, 1)
        both = tails[:, 0] + moved.reshape(nz, ng // 2, LANES)
        return jnp.concatenate([flat[0].reshape(nz, ng, LANES), both], axis=1).astype(BF16)

    def unfold(block):
        both = block[:, ng:].astype(F32)
        moved = pltpu.roll(both.reshape(rows // 2, LANES), 2 * LANES - width, 1).reshape(nz, ng // 2, LANES)
        flat[0] = block[:, :ng].astype(F32).reshape(rows, LANES)
        flat[1, :, : width - LANES] = jnp.concatenate([both, moved], axis=1).reshape(rows, LANES)[:, : width - LANES]

    for k in range(2):
        loads[k].wait()
        put_rows(xt[k].T)
        xs[k] = fold()
    for load in loads[2:]:
        load.wait()
    wide_in = jnp.zeros((PAD - width, win.shape[1]), BF16)
    wi[:width] = win[:width]
    wi[width:PAD] = wide_in
    wi[PAD : PAD + width] = win[width:]
    wi[PAD + width :] = wide_in
    wit[...] = wi[...].T
    wo[...] = widen(wout[...].astype(F32), width).astype(BF16)
    wot[...] = wo[...].T
    gate[...] = jax.nn.sigmoid(widen(jnp.broadcast_to(logit_row[...].reshape(1, 2 * width), (8, 2 * width)), width))
    scale[...] = widen(jnp.broadcast_to(scale_row[...].reshape(1, 2 * width), (8, 2 * width)), width)
    bias = bias_row[...].reshape(1, bias_row.shape[0])
    lane = lax.broadcasted_iota(jnp.int32, (1, 2 * PAD), 1) % PAD
    mask = jnp.where(lane < width, 1.0, 0.0)

    pl.semaphore_wait(barrier, (nz - 1) + (ng - 1))

    def send(src, dst, send_sem, recv_sem, device):
        return pltpu.make_async_remote_copy(
            src_ref=src, dst_ref=dst, send_sem=send_sem, recv_sem=recv_sem,
            device_id=(device,), device_id_type=pl.DeviceIdType.MESH,
        )

    def bytes_of(ref, sem):
        return pltpu.make_async_copy(ref, ref, sem)

    def each(count, copy, landing, recv_sem):
        def start():
            @pl.loop(1, count)
            def _(j):
                copy(j).start()

        return start, bytes_of(landing.at[pl.ds(0, count - 1)], recv_sem).wait

    def exchange(count, place, src, dst, send_sem, recv_sem, device_of):
        def copy(j):
            to = lax.rem(place + j, count)
            return send(src.at[to], dst.at[place], send_sem, recv_sem, device_of(to))

        return each(count, copy, dst, recv_sem)

    def exchange_with(targets, place, src, dst, send_sem, recv_sem):
        def start():
            for to, device in targets:
                send(src.at[to], dst.at[place], send_sem, recv_sem, device).start()

        return start, bytes_of(dst.at[pl.ds(0, len(targets))], recv_sem).wait

    def spread_with(targets, place, ref, send_sem, recv_sem):
        def start():
            for _, device in targets:
                send(ref.at[place], ref.at[place], send_sem, recv_sem, device).start()

        return start, bytes_of(ref.at[pl.ds(0, len(targets))], recv_sem).wait

    def start_a(k):
        start, wait = exchange_with(z_targets, z, xs.at[k], ra.at[k], a_send, a_recv.at[k])
        start()
        ra[k, z] = xs[k, z]
        return wait

    def strided(start, size, stride):
        return jnp.concatenate([flat[h, pl.ds(start, size, stride=stride), :] for h in range(2)], axis=1)

    def start_b(k):
        unfold(ra[k])
        for g in range(ng):
            tb[k, g] = strided(g, nz, ng)[:, :width].astype(BF16)
        start, wait = exchange_with(group_targets, group, tb.at[k], rb.at[k], b_send, b_recv.at[k])
        start()
        rb[k, group] = tb[k, group]
        return wait

    wait_a0 = start_a(0)
    wait_a1 = start_a(1)
    wait_a0()
    wait_b0 = start_b(0)
    wait_a1()
    wait_b1 = start_b(1)
    wait_b0()

    def load_state(k):
        put_rows(rb[k])
        return jnp.concatenate([flat[0], flat[1]], axis=1)

    def swap_order(state, major, minor):
        flat[0] = state[:, :LANES]
        flat[1] = state[:, LANES:]
        return jnp.concatenate([strided(j, major, minor) for j in range(minor)], axis=0)

    def block_of(level):
        if level < low_levels:
            return nz * 2**level
        return ng * 2 ** (level - low_levels) if level < mid_levels else ns * 2 ** (level - mid_levels)

    state = load_state(0)
    for level in range(levels):
        if level == low_levels:
            state = swap_order(state, ng, nz)
        first, second = halves(state, block_of(level))
        paired = jnp.concatenate([first, second], axis=1)
        average = jnp.sum(paired, axis=1, keepdims=True) * (1.0 / (2 * width))
        centered = paired - average * mask
        inverse = lax.rsqrt(jnp.sum(centered * centered, axis=1, keepdims=True) * (1.0 / (2 * width)) + epsilon)
        normed = centered * inverse
        nrm[level] = normed
        inv[level] = inverse
        here = pl.ds(level * pairs, pairs)
        nlc[here, :] = narrow(normed[:, :PAD], normed[:, PAD:], width).astype(BF16)
        preact = row_dot(normed.astype(BF16), wi[...]) + bias
        square = preact * preact
        tangent = jnp.tanh(preact * (tanh_scale + (tanh_scale * cubic_coef) * square))
        half = 0.5 + 0.5 * tangent
        product = preact * half
        activated = product.astype(BF16)
        act[here, :] = activated
        slope[level] = half + (product - product * half) * (
            (2.0 * tanh_scale) + (6.0 * tanh_scale * cubic_coef) * square
        )
        if level + 1 < levels:
            result = gate[0:1] * paired + scale[0:1] * row_dot(activated, wo[...])
            state = unite(result[:, :PAD], result[:, PAD:], block_of(level))

    chunks = gb.shape[0]
    half_chunks = chunks // 2
    span = 2 * width
    units = act.shape[1]
    in_rows, out_rows = span // half_chunks, units // half_chunks
    to_sibling = []

    def start_c(k):
        to_sibling.append(send(gb.at[k, 1 - c], rc.at[k], c_send, c_recv.at[k], sibling))
        to_sibling[k].start()

    plane_waits = []

    def start_d(k):
        to_sibling[k].wait_recv()
        hsum[k] = gb[k, c] + rc[k]
        start, wait = exchange_with(plane_targets, plane, hsum.at[k], rd.at[k], d_send, d_recv.at[k])
        start()
        plane_waits.append(wait)
        rd[k, plane] = hsum[k, plane]

    wait_b1()
    state = swap_order(load_state(1), ng, nz)
    for level in reversed(range(levels)):
        if level == low_levels - 1:
            state = swap_order(state, nz, ng)
        first, second = halves(state, block_of(level))
        upstream = jnp.concatenate([first, second], axis=1)
        branch = scale[0:1] * upstream
        here = pl.ds(level * pairs, pairs)
        bgc[here, :] = narrow(branch[:, :PAD], branch[:, PAD:], width).astype(BF16)
        if level == 0:
            grad_out = column_dot(act[...], bgc[...])
            for k in range(half_chunks):
                gb[k] = grad_out[k * out_rows : (k + 1) * out_rows].reshape(2, npl, 8, span).astype(BF16)
                start_c(k)
        preact_grad = (row_dot(branch.astype(BF16), wot[...]) * slope[level]).astype(BF16)
        pg[here, :] = preact_grad
        if level == 0:
            for k in range(half_chunks):
                start_d(k)
            grad_in = column_dot(nlc[...], pg[...])
            for k in range(half_chunks):
                for h in range(2):
                    part = grad_in[k * in_rows : (k + 1) * in_rows, h * span : (h + 1) * span]
                    gb[half_chunks + k, h] = part.reshape(npl, 8, span).astype(BF16)
                start_c(half_chunks + k)
        normed_grad = row_dot(preact_grad, wit[...])
        normed = nrm[level]
        mean_grad = jnp.sum(normed_grad, axis=1, keepdims=True) * (1.0 / (2 * width))
        mean_both = jnp.sum(normed_grad * normed, axis=1, keepdims=True) * (1.0 / (2 * width))
        grad = gate[0:1] * upstream + inv[level] * (normed_grad - mean_grad * mask - normed * mean_both)
        state = unite(grad[:, :PAD], grad[:, PAD:], block_of(level))

    tx[...] = state[:, :width].reshape(ng, nz, width).astype(BF16)
    start_u, wait_u = exchange(ng, group, tx, rx1, u_send, u_recv, id_group)
    for k in range(half_chunks, chunks):
        start_d(k)
    start_u()
    rx1[group] = tx[group]

    def added(ref, count):
        total = ref[0].astype(F32)
        for i in range(1, count):
            total = total + ref[i].astype(F32)
        return total

    z_waits = []
    for k in range(chunks):
        plane_waits[k]()
        rz[k, z] = added(rd.at[k], npl).astype(BF16)
        start, wait = spread_with(z_targets, z, rz.at[k], z_send, z_recv.at[k])
        start()
        z_waits.append(wait)

    def return_rows():
        wait_u()
        put_rows(rx1[...])
        for j in range(nz):
            tx2[j] = strided(j, ng, nz)[:, :width].astype(BF16)
        start_v, wait_v = exchange(nz, z, tx2, rx2, v_send, v_recv, id_z)
        start_v()
        rx2[z] = tx2[z]
        return wait_v

    gather_waits = []
    for k in range(chunks):
        z_waits[k]()
        rg[k, c, plane] = (added(rz.at[k], nz) * scale_out).astype(BF16)
        start, wait = spread_with(plane_targets, plane, rg.at[k, c], e_send, e_recv.at[k])
        start()
        gather_waits.append(wait)
        if k == chunks - 2:
            wait_v = return_rows()
    over = []

    for k in range(chunks):
        gather_waits[k]()
        over.append(send(rg.at[k, c], rg.at[k, c], f_send, f_recv.at[k], sibling))
        over[k].start()
    wait_v()
    for k in range(chunks):
        over[k].wait_recv()

    bytes_of(xs.at[:, pl.ds(0, nz - 1)], a_send).wait()
    bytes_of(tb.at[:, pl.ds(0, ng - 1)], b_send).wait()
    bytes_of(rc, c_send).wait()
    bytes_of(hsum.at[:, pl.ds(0, npl - 1)], d_send).wait()
    bytes_of(rz.at[:, pl.ds(0, nz - 1)], z_send).wait()
    bytes_of(hsum.at[:, pl.ds(0, npl - 1)], e_send).wait()
    bytes_of(rc, f_send).wait()
    bytes_of(tx.at[pl.ds(0, ng - 1)], u_send).wait()
    bytes_of(tx2.at[pl.ds(0, nz - 1)], v_send).wait()


def finish(gx, grads, gxt_hbm, gin_hbm, gout_hbm, gxt, gin, gout, out_sem):
    half_chunks = grads.shape[0] // 2
    span, units = gin.shape
    in_rows, out_rows = span // half_chunks, units // half_chunks
    for k in range(half_chunks):
        here = pl.ds(k * out_rows, out_rows)
        gout[here, :] = grads[k].astype(F32).reshape(out_rows, span)
        pltpu.make_async_copy(gout.at[here], gout_hbm.at[here], out_sem.at[0]).start()
    for k in range(half_chunks):
        here = pl.ds(k * in_rows, in_rows)
        for h in range(2):
            gin[here, h * span : (h + 1) * span] = grads[half_chunks + k, h].astype(F32).reshape(in_rows, span)
        pltpu.make_async_copy(gin.at[here], gin_hbm.at[here], out_sem.at[1]).start()
    gxt[...] = gx[...].reshape(gxt.shape[1], gxt.shape[0]).T
    last = pltpu.make_async_copy(gxt, gxt_hbm, out_sem.at[2])
    last.start()
    pltpu.make_async_copy(gout, gout_hbm, out_sem.at[0]).wait()
    pltpu.make_async_copy(gin, gin_hbm, out_sem.at[1]).wait()
    last.wait()


def build(mesh, dims):
    ny, nz, nx, nc = dims
    npl, ng = ny * nx, ny * nx * nc
    rows, pairs = nz * ng, nz * ng // 2
    levels = rows.bit_length() - 1

    def step(saved_input, cotangent, w_in, bias_in, w_out, residual_logit, branch_scale):
        width, units = saved_input.shape[1], w_in.shape[1]
        span = 2 * width
        half_chunks = span // (npl * 8)
        chunks = 2 * half_chunks
        vmem = pltpu.VMEM
        dma = pltpu.SemaphoreType.DMA
        scratch = [
            vmem((2, width, rows), BF16),
            vmem((span, units), BF16),
            vmem((units,), F32),
            vmem((units, span), BF16),
            vmem((span,), F32),
            vmem((span,), F32),
            vmem((2, nz, ng + ng // 2, LANES), BF16),
            vmem((2, nz, ng + ng // 2, LANES), BF16),
            vmem((2, ng, nz, width), BF16),
            vmem((2, ng, nz, width), BF16),
            vmem((2, rows, LANES), F32),
            vmem((2 * PAD, units), BF16),
            vmem((units, 2 * PAD), BF16),
            vmem((units, 2 * PAD), BF16),
            vmem((2 * PAD, units), BF16),
            vmem((8, 2 * PAD), F32),
            vmem((8, 2 * PAD), F32),
            vmem((levels, pairs, 2 * PAD), F32),
            vmem((levels, pairs, 1), F32),
            vmem((levels, pairs, units), F32),
            vmem((levels * pairs, span), BF16),
            vmem((levels * pairs, units), BF16),
            vmem((levels * pairs, units), BF16),
            vmem((levels * pairs, span), BF16),
            vmem((chunks, 2, npl, 8, span), BF16),
            vmem((chunks, npl, 8, span), BF16),
            vmem((chunks, npl, 8, span), BF16),
            vmem((chunks, npl, 8, span), BF16),
            vmem((chunks, nz, 8, span), BF16),
            vmem((ng, nz, width), BF16),
            vmem((ng, nz, width), BF16),
            vmem((nz, ng, width), BF16),
            dma((7,)),
            dma, dma((2,)),
            dma, dma((2,)),
            dma, dma((chunks,)),
            dma, dma((chunks,)),
            dma, dma((chunks,)),
            dma, dma((chunks,)),
            dma, dma((chunks,)),
            dma, dma,
            dma, dma,
        ]
        in_vmem = pl.BlockSpec(memory_space=pltpu.VMEM)
        gx, grads = pl.pallas_call(
            functools.partial(kernel, dims, float(rows * rows) ** (-0.5)),
            out_shape=(vmem((nz, ng, width), BF16), vmem((chunks, 2, npl, 8, span), BF16)),
            in_specs=[pl.BlockSpec(memory_space=pl.ANY)] * 7,
            out_specs=(in_vmem, in_vmem),
            scratch_shapes=scratch,
            compiler_params=pltpu.CompilerParams(collective_id=0, has_side_effects=True, vmem_limit_bytes=60 * 2**20),
        )(saved_input.T, cotangent.T, w_in, bias_in, w_out, residual_logit, branch_scale)
        gxt, grad_in, grad_out = pl.pallas_call(
            finish,
            out_shape=(
                jax.ShapeDtypeStruct((width, rows), BF16),
                jax.ShapeDtypeStruct((span, units), F32),
                jax.ShapeDtypeStruct((units, span), F32),
            ),
            in_specs=[in_vmem] * 2,
            out_specs=(pl.BlockSpec(memory_space=pl.ANY),) * 3,
            scratch_shapes=[
                vmem((width, rows), BF16), vmem((span, units), F32), vmem((units, span), F32), dma((3,)),
            ],
            compiler_params=pltpu.CompilerParams(vmem_limit_bytes=48 * 2**20),
        )(gx, grads)
        return gxt.T, grad_in, grad_out

    in_specs = (P("seq", None), P("seq", None), P(), P(), P(), P(), P())
    out_specs = (P("seq", None), P(), P())
    return jax.shard_map(step, mesh=mesh, in_specs=in_specs, out_specs=out_specs, check_vma=False)


def solution(mesh):
    return build(mesh, (4, 8, 4, 2))
```
